32 devices in a mesh: lists: 4 (over y, x), points: 8 (over z, core).
Axes of the slice: x: 2, y: 2, z: 4, core: 2. Of those that a mesh axis runs over, the one named last changes fastest.
Arguments:
- child_centroids: float32 [1024, 768], P(('lists', 'points')), may hold values from -6 to 6
- child_sizes: int32 [1024], P(('lists', 'points')), may hold values from 1 to 256
- parent_of: int32 [1024], P(('lists', 'points')), may hold values from 0 to 511, as said below
- points: bfloat16 [49152, 768], P(('lists', 'points')), may hold values from -6 to 6
- assign: int32 [49152], P(('lists', 'points')), may hold values from 0 to 127
- codes: int32 [49152, 96], P(('lists', 'points')), may hold values from 0 to 255
- rotation: bfloat16 [768, 768], replicated, may hold values from -0.21875 to 0.21875
Outputs:
- merged_centroids: float32 [512, 768], P(('lists', 'points'))
- codeword_means: float32 [768, 256], replicated
The draws below stay inside these ranges and needn't reach their ends.
Inputs may be any that keep to these rules, and one draw needn't show every extreme that they name: `parent_of`: every parent has exactly two children. Of the 32 children of one device, at most 16 have parents in one block of 128 consecutive parent numbers, and exactly 16 in some block.
All inputs are finite; a program needn't handle non-finite values.
Results may differ from the reference program's by a relative error of at most 0.0042.
Values may be sent and summed in bfloat16 or wider, within the bound.
No kernel may reach another device: no remote copies, remote signals or barrier semaphores. Data moves between devices by JAX's collectives and lax.ppermute only.
A program may use at most 64 MiB of HBM per device.

```python
import math
import jax
import jax.numpy as jnp
import numpy as np
from jax import lax

D = 768
SUBS = 96
CODEWORDS = 256
CH_DEV = 32
PTS_DEV = 1536
SUBDIM = 8
CHILDREN = 1024
PARENTS = 512
OWNERS = 4
PAR_DEV = 128
CAP = 16
POINTS = 49152
PTS_LIST = 12288


def draw_parent_of(key, part):
    owners = OWNERS
    groups = CHILDREN // CH_DEV
    loads = np.zeros(owners, np.int64)
    loads[0] = CAP
    remain = CH_DEV - CAP
    spread = remain // (owners - 1)
    extra = remain - spread * (owners - 1)
    for index in range(1, owners):
        loads[index] = spread + (1 if index <= extra else 0)
    slot_owner = jnp.asarray(np.repeat(np.arange(owners), loads).astype(np.int32))
    key_roll = jax.random.fold_in(key, 11)
    key_local = jax.random.fold_in(key, 12)
    key_pairs = jax.random.fold_in(key, 13)
    shift_by = jax.random.randint(key_roll, (), 0, owners, dtype=jnp.int32)
    device_ids = jnp.arange(groups, dtype=jnp.int32)
    owner_table = (slot_owner[None, :] + device_ids[:, None] + shift_by) % owners
    orders = jax.vmap(lambda sub_key: jax.random.permutation(sub_key, CH_DEV))(jax.random.split(key_local, groups))
    owner_table = jnp.take_along_axis(owner_table, orders.astype(jnp.int32), axis=1).reshape(CHILDREN)
    membership = (owner_table[:, None] == jnp.arange(owners, dtype=jnp.int32)[None, :]).astype(jnp.int32)
    slot_rank = jnp.sum(jnp.cumsum(membership, axis=0) * membership, axis=1) - 1
    pairings = jax.vmap(lambda sub_key: jax.random.permutation(sub_key, 2 * PAR_DEV))(jax.random.split(key_pairs, owners)).astype(jnp.int32)
    placed = pairings[owner_table, slot_rank]
    return (owner_table * PAR_DEV + placed // 2).astype(jnp.int32)


def touch_ends(drawn, rng, least, largest):
    longest = drawn.shape.index(max(drawn.shape))
    spots = []
    for shift in (0, 1):
        where = [jax.random.randint(jax.random.fold_in(rng, axis), (), 0, length) for axis, length in enumerate(drawn.shape)]
        where[longest] = (where[longest] + shift) % drawn.shape[longest]
        spots.append(tuple(where))
    return drawn.at[spots[0]].set(least).at[spots[1]].set(largest)


def shard_levels(key, extent, cuts, low, high):
    factor_of = 1.0
    for dim, parts in cuts:
        heights = jax.random.uniform(jax.random.fold_in(jax.random.fold_in(key, 6), dim), (parts,), jnp.float32, low / len(cuts), high / len(cuts))
        factor_of = factor_of * jnp.repeat(jnp.exp(heights), extent[dim] // parts).reshape((-1,) + (1,) * (len(extent) - 1 - dim))
    return factor_of


def cumulative_ranks(amount, skew):
    weights = [(1 << 20) // math.isqrt(grade ** skew) + 1 for grade in range(1, amount + 1)]
    scale = 1 + sum(weights) // (1 << 30)
    return np.cumsum(np.array([max(1, weight // scale) for weight in weights]))


def ranked(own_key, dims, number_of, skew):
    grid = cumulative_ranks(number_of, skew)
    lot = jax.random.randint(jax.random.fold_in(own_key, 1), dims, 0, int(grid[number_of - 1]))
    rank = jnp.searchsorted(jnp.asarray(grid, jnp.int32), lot, side="right")
    return jax.random.permutation(jax.random.fold_in(own_key, 2), number_of)[rank].astype(jnp.int32)


def centred(own_key, dims, scale, most, shards=(), kind=jnp.bfloat16):
    level = shard_levels(own_key, dims, shards, -0.22, 0.18) if shards else 1.0
    values = jax.random.normal(own_key, dims, jnp.float32) * scale * level
    return jnp.minimum(jnp.maximum(values, -most), most).astype(kind)


def setup_inputs(seed: int = 0) -> dict:
    streams_of = jax.random.split(jax.random.key(seed), 8)
    return {
        "child_centroids": centred(streams_of[0], (CHILDREN, D), 1.0, 6.0, ((0, 32),), jnp.float32),
        "child_sizes": touch_ends(jax.random.randint(streams_of[1], (CHILDREN,), 1, 257), jax.random.fold_in(streams_of[1], 1), 1, 256).astype(jnp.int32),
        "parent_of": draw_parent_of(jax.random.fold_in(streams_of[7], 71), 0),
        "points": centred(streams_of[3], (POINTS, D), 1.0, 6.0, ((0, 32),)),
        "assign": touch_ends(ranked(streams_of[4], (POINTS,), PAR_DEV, 2), jax.random.fold_in(streams_of[4], 3), 0, PAR_DEV - 1).astype(jnp.int32),
        "codes": touch_ends(jax.random.randint(streams_of[5], (POINTS, SUBS), 0, CODEWORDS), jax.random.fold_in(streams_of[5], 1), 0, CODEWORDS - 1).astype(jnp.int32),
        "rotation": centred(streams_of[6], (D, D), D ** -0.5, 0.21875),
    }


def reference(child_centroids, child_sizes, parent_of, points, assign, codes, rotation):
    child_weight = child_sizes.astype(jnp.float32)
    weighted = child_weight[:, None] * child_centroids
    parent_sum = jax.ops.segment_sum(weighted, parent_of, num_segments=PARENTS)
    parent_mass = jax.ops.segment_sum(child_weight, parent_of, num_segments=PARENTS)
    merged = parent_sum / parent_mass[:, None]
    lowered = merged.astype(jnp.bfloat16)
    blocks = POINTS // PTS_DEV
    position = jnp.arange(POINTS, dtype=jnp.int32)
    parent_id = ((position // PTS_LIST) * PAR_DEV + assign).astype(jnp.int32)
    codeword_ids = jnp.arange(CODEWORDS, dtype=jnp.int32)

    def accumulate(carried, block_inputs):
        code_sums, code_counts = carried
        point_blk, parent_blk, code_blk = block_inputs
        chosen = jnp.take(lowered, parent_blk, axis=0)
        residual = (point_blk.astype(jnp.float32) - chosen.astype(jnp.float32)).astype(jnp.bfloat16)
        rotated = jnp.dot(residual, rotation, preferred_element_type=jnp.float32).astype(jnp.bfloat16)
        onehot = (code_blk[:, :, None] == codeword_ids[None, None, :]).astype(jnp.float32)
        pieces = rotated.astype(jnp.float32).reshape(-1, SUBS, SUBDIM)
        code_sums = code_sums + jnp.einsum("pmd,pmk->mdk", pieces, onehot, precision=lax.Precision.HIGHEST)
        code_counts = code_counts + jnp.sum(onehot, axis=0)
        return (code_sums, code_counts), None

    initial = (jnp.zeros((SUBS, SUBDIM, CODEWORDS), jnp.float32), jnp.zeros((SUBS, CODEWORDS), jnp.float32))
    (code_sums, code_counts), _ = lax.scan(accumulate, initial, (points.reshape(blocks, PTS_DEV, D), parent_id.reshape(blocks, PTS_DEV), codes.reshape(blocks, PTS_DEV, SUBS)))
    means = code_sums / (1.0 + code_counts[:, None, :])
    return merged, means.reshape(D, CODEWORDS)
```

```python
import math

import jax
import jax.numpy as jnp
from jax import lax
from jax.experimental import pallas as pl
from jax.experimental.pallas import tpu as pltpu
from jax.sharding import PartitionSpec as P

CODEWORDS = 256
LOW = 32
HIGH = CODEWORDS // LOW
GROUP = 3
UNROLL = 8
LANES = 128
SWAP = ((0, 1), (1, 0))


def dot_nt(a, b):
    return lax.dot_general(a, b, (((1,), (1,)), ((), ())), preferred_element_type=jnp.float32)


def code_kernel(points_ref, assign_ref, codes_ref, rotation_ref, lowered_ref, out_ref, rot_ref, rest_ref, turned_ref):
    width, count = rot_ref.shape
    parents = lowered_ref.shape[0]
    sub_width = width // codes_ref.shape[0]
    groups = out_ref.shape[0]
    turned_ref[...] = rotation_ref[...].T
    piece = count // 3

    @pl.loop(0, 3)
    def _(step):
        span = pl.ds(pl.multiple_of(step * piece, piece), piece)
        parent_ids = lax.broadcasted_iota(jnp.int32, (parents, piece), 0)
        pick = jnp.where(parent_ids == assign_ref[:, span], 1.0, 0.0).astype(jnp.bfloat16)
        chosen = lax.dot_general(
            pick, lowered_ref[...], (((0,), (0,)), ((), ())), preferred_element_type=jnp.float32
        )
        rest_ref[span, :] = (points_ref[span, :].astype(jnp.float32) - chosen).astype(jnp.bfloat16)

    rows = width // 2

    @pl.loop(0, 2)
    def _(block):
        span = pl.ds(pl.multiple_of(block * rows, rows), rows)
        turned = turned_ref[span, :]
        for step in range(3):
            part = slice(step * piece, (step + 1) * piece)
            rotated = dot_nt(turned, rest_ref[part, :])
            rot_ref[span, part] = rotated.astype(jnp.bfloat16).astype(jnp.float32)

    def small(ids):
        return ids.astype(jnp.float32).astype(jnp.bfloat16)

    low_ids = small(lax.broadcasted_iota(jnp.int32, (LOW, count), 0))
    pair_ids = small(lax.broadcasted_iota(jnp.int32, (2 * sub_width, count), 0) // sub_width)
    high_ids = lax.broadcasted_iota(jnp.int32, (HIGH, count), 0)
    quarter = lax.broadcasted_iota(jnp.int32, (8, LANES), 1) // LOW
    line = lax.broadcasted_iota(jnp.int32, (8, LANES), 0)
    wide_line = lax.broadcasted_iota(jnp.int32, (8, CODEWORDS), 0)
    one, zero = jnp.ones((), jnp.bfloat16), jnp.zeros((), jnp.bfloat16)

    def moved(block, sub, place):
        turn = ((place - sub) * LOW) % LANES
        return pltpu.roll(block, turn, 1) if turn else block

    def one_group(group):
        weights, masked, tallies = [], [], []
        for sub in range(GROUP):
            index = group * GROUP + sub
            code = codes_ref[pl.ds(index, 1), :]
            low = small(jnp.broadcast_to(code & (LOW - 1), (LOW, count)))
            weights.append(jnp.where(low_ids == low, one, zero))
            high = code >> 5
            value = rot_ref[pl.ds(pl.multiple_of(index * sub_width, sub_width), sub_width), :]
            value = jnp.concatenate([value, value], axis=0).astype(jnp.bfloat16)
            behind = small(jnp.broadcast_to(high, (2 * sub_width, count))) - pair_ids
            for k in range(0, HIGH, 2):
                masked.append(jnp.where(behind == jnp.asarray(k, jnp.bfloat16), value, zero))
            tallies.append(jnp.where(high_ids == jnp.broadcast_to(high, (HIGH, count)), 1.0, 0.0))
        tallies.append(jnp.zeros((8, count), jnp.float32))
        weights.append(jnp.zeros((LANES - GROUP * LOW, count), jnp.bfloat16))
        result = dot_nt(
            jnp.concatenate(masked + [jnp.concatenate(tallies, axis=0).astype(jnp.bfloat16)], axis=0),
            jnp.concatenate(weights, axis=0),
        )
        lines = []
        for sub in range(GROUP):
            halves = []
            for half in range(2):
                total = None
                for place in range(4):
                    start = (sub * HIGH + half * 4 + place) * sub_width
                    part = jnp.where(quarter == place, moved(result[start : start + sub_width], sub, place), 0.0)
                    total = part if total is None else total + part
                halves.append(total)
            lines.append(jnp.concatenate(halves, axis=1))
        counts = jnp.zeros((8, CODEWORDS), jnp.float32)
        for sub in range(GROUP):
            start = GROUP * HIGH * sub_width + sub * HIGH
            block = result[start : start + HIGH]
            halves = []
            for half in range(2):
                total = None
                for place in range(4):
                    keep = (quarter == place) & (line == half * 4 + place)
                    part = jnp.where(keep, moved(block, sub, place), 0.0)
                    total = part if total is None else total + part
                halves.append(jnp.sum(total, axis=0, keepdims=True))
            row = jnp.broadcast_to(jnp.concatenate(halves, axis=1), (8, CODEWORDS))
            counts = jnp.where(wide_line == sub, row, counts)
        out_ref[group] = jnp.concatenate(lines + [counts], axis=0)

    @pl.loop(0, groups // UNROLL)
    def _(step):
        for k in range(UNROLL):
            one_group(step * UNROLL + k)


def code_sums(points, assign, codes, rotation, lowered):
    count, width = points.shape
    groups = codes.shape[0] // GROUP
    rows = GROUP * (width // codes.shape[0]) + 8
    return pl.pallas_call(
        code_kernel,
        out_shape=jax.ShapeDtypeStruct((groups, rows, CODEWORDS), jnp.float32),
        in_specs=[pl.BlockSpec(memory_space=pltpu.VMEM)] * 5,
        out_specs=pl.BlockSpec(memory_space=pltpu.VMEM),
        scratch_shapes=[
            pltpu.VMEM((width, count), jnp.float32),
            pltpu.VMEM((count, width), jnp.bfloat16),
            pltpu.VMEM((width, width), jnp.bfloat16),
        ],
        compiler_params=pltpu.CompilerParams(vmem_limit_bytes=48 << 20),
    )(points, assign, codes, rotation, lowered)


def body(child_centroids, child_sizes, parent_of, points, assign, codes, rotation):
    lists, rings = lax.axis_size("lists"), lax.axis_size("z")
    chips = lists * rings
    core = lax.axis_index("core")
    child_count, width = child_centroids.shape
    owner_parents = rings * child_count
    shard_rows = child_count // 2
    most = child_count // math.isqrt(lists)

    size = child_sizes[:, None]
    parent = parent_of[:, None]
    digits = jnp.concatenate([size >> 4, size & 15, parent >> 8, parent & 255], axis=1).astype(jnp.float32)
    sent = jnp.concatenate(
        [size.astype(jnp.float32) * child_centroids, jnp.pad(digits, ((0, 0), (0, LANES - 4)))], axis=1
    ).astype(jnp.bfloat16)
    owner = parent_of // owner_parents
    ids = jnp.arange(child_count, dtype=jnp.int32)
    earlier = (owner[:, None] == owner[None, :]) & (ids[None, :] < ids[:, None])
    slot = owner * most + jnp.sum(earlier, axis=1, dtype=jnp.int32)
    slots = jnp.arange(lists * most, dtype=jnp.int32)
    pack = (slots[:, None] == slot[None, :]).astype(jnp.bfloat16)
    packed = jnp.dot(pack, sent, preferred_element_type=jnp.float32).astype(jnp.bfloat16)
    packed = packed.reshape(lists, 1, most, width + LANES)
    packed = jnp.broadcast_to(packed, (lists, rings, most, width + LANES)).reshape(chips, most, width + LANES)
    near = lax.all_to_all(packed, ("lists", "z"), 0, 0).reshape(chips * most, width + LANES)
    near_parent = (near[:, width + 2].astype(jnp.int32) << 8) + near[:, width + 3].astype(jnp.int32)
    wanted = lax.axis_index("lists") * owner_parents + jnp.arange(owner_parents, dtype=jnp.int32)
    pick = (wanted[:, None] == near_parent[None, :]).astype(jnp.bfloat16)
    partial = jnp.dot(pick, near, preferred_element_type=jnp.float32)
    whole = partial + lax.ppermute(partial.astype(jnp.bfloat16), "core", SWAP).astype(jnp.float32)
    mass = whole[:, width] * 16.0 + whole[:, width + 1]
    merged_all = whole[:, :width] / mass[:, None]
    lowered = merged_all.astype(jnp.bfloat16)
    shard = lax.axis_index("z") * 2 + core
    merged = lax.dynamic_slice_in_dim(merged_all, shard * shard_rows, shard_rows, 0)

    sums = code_sums(points, assign[None, :], codes.T, rotation, lowered)
    groups, rows, _ = sums.shape
    half_groups = groups // 2
    splits = chips // half_groups
    sums = sums.reshape(2, half_groups, rows, splits, CODEWORDS // splits)
    sums = sums.transpose(0, 1, 3, 2, 4).reshape(2, chips, rows, CODEWORDS // splits)
    kept = lax.dynamic_index_in_dim(sums, core, 0, keepdims=False)
    given = lax.dynamic_index_in_dim(sums, 1 - core, 0, keepdims=False)
    taken = lax.ppermute(given, "core", SWAP)
    chip = (kept.astype(jnp.float32) + taken.astype(jnp.float32)).astype(jnp.bfloat16)
    total = jnp.sum(lax.all_to_all(chip, ("lists", "z"), 0, 0).astype(jnp.float32), axis=0)
    sub_width = (rows - 8) // GROUP
    tops = total[: rows - 8].reshape(GROUP, sub_width, -1)
    means = tops / (1.0 + total[rows - 8 : rows - 8 + GROUP, None, :])
    means = means.reshape(1, rows - 8, -1).astype(jnp.bfloat16)
    means = jnp.broadcast_to(means, (chips,) + means.shape[1:])
    mine = lax.all_to_all(means, ("lists", "z"), 0, 0)
    mine = mine.reshape(half_groups, splits, rows - 8, -1).transpose(0, 2, 1, 3).reshape(-1, CODEWORDS)
    other = lax.ppermute(mine, "core", SWAP)
    first = core == 0
    whole = jnp.concatenate([jnp.where(first, mine, other), jnp.where(first, other, mine)], axis=0)
    return merged, whole.astype(jnp.float32)


def solution(mesh):
    lists, points = mesh.devices.shape
    split = jax.sharding.Mesh(mesh.devices.reshape(lists, points // 2, 2), ("lists", "z", "core"))
    every = ("lists", "z", "core")
    in_specs = (P(every, None), P(every), P(every), P(every, None), P(every), P(every, None), P())
    out_specs = (P(every, None), P())
    return jax.shard_map(body, mesh=split, in_specs=in_specs, out_specs=out_specs, check_vma=False)
```

```python
import functools
import math

import jax
import jax.numpy as jnp
from jax import lax
from jax.experimental import pallas as pl
from jax.experimental.pallas import tpu as pltpu
from jax.sharding import PartitionSpec as P

CODEWORDS = 256
LOW = 32
HIGH = CODEWORDS // LOW
GROUP = 3
SIDE = 8
UNROLL = 3
FRACTION = 14.0
SIZE_BITS, PARENT_BITS, EXPONENT_BITS = 9, 13, 8
SLABS = 4
PIECES = 3
BLOCKS = 2
LANES = 128

FULL = 66_900_000
MOST = 66_200_000
SOME = 50_000_000
SWAP = ((0, 1), (1, 0))


def dot_nt(a, b):
    return lax.dot_general(a, b, (((1,), (1,)), ((), ())), preferred_element_type=jnp.float32)


def as_column(row):
    count = row.shape[1]
    shape = (count, count)
    here = lax.broadcasted_iota(jnp.int32, shape, 0) == lax.broadcasted_iota(jnp.int32, shape, 1)
    return jnp.sum(jnp.where(here, jnp.broadcast_to(row, shape), 0), axis=1, keepdims=True)


def power(exponent):
    return jnp.exp2(exponent)


def pack_kernel(owner_parents, child_hbm, size_hbm, parent_hbm, out_ref, child_ref, size_ref, parent_ref, sems):
    copies = [
        pltpu.make_async_copy(source, target, sems.at[k])
        for k, (source, target) in enumerate(
            ((child_hbm, child_ref), (size_hbm, size_ref), (parent_hbm, parent_ref))
        )
    ]
    for copy in copies:
        copy.start()
    for copy in copies:
        copy.wait()
    lists, rings, most, width = out_ref.shape
    count = child_ref.shape[0]
    parent_row = parent_ref[...]
    parent = as_column(parent_row)
    size = as_column(size_ref[...])
    owner_row, owner = parent_row // owner_parents, parent // owner_parents
    shape = (count, count)
    before = lax.broadcasted_iota(jnp.int32, shape, 0) < lax.broadcasted_iota(jnp.int32, shape, 1)
    earlier = jnp.where((owner == owner_row) & before, 1, 0)
    slot = owner_row * most + jnp.sum(earlier, axis=0, keepdims=True)
    slots = lax.broadcasted_iota(jnp.int32, (lists * most, count), 0)
    pack = jnp.where(slots == slot, 1.0, 0.0).astype(jnp.bfloat16)
    child = child_ref[...]
    top = jnp.max(jnp.abs(child), axis=1, keepdims=True)
    exponent = jnp.ceil(jnp.log2(jnp.maximum(top, 1e-30)))
    scaled = jnp.floor(child * power(FRACTION - exponent) + 0.5)
    word = size + (parent << SIZE_BITS)
    word = word + ((exponent.astype(jnp.int32) + 128) << (SIZE_BITS + PARENT_BITS))
    lane = lax.broadcasted_iota(jnp.int32, (count, LANES), 1)
    bit = (jnp.broadcast_to(word, (count, LANES)) >> jnp.minimum(lane, 31)) & 1
    marked = 2.0 * jnp.floor(scaled[:, :LANES] * 0.5) + bit.astype(jnp.float32)
    sent = jnp.concatenate([marked, scaled[:, LANES:]], axis=1)
    upper = jnp.floor(sent * (1.0 / 128.0))
    lower = sent - upper * 128.0
    packed = 128.0 * jnp.dot(pack, upper.astype(jnp.bfloat16), preferred_element_type=jnp.float32)
    packed = packed + jnp.dot(pack, lower.astype(jnp.bfloat16), preferred_element_type=jnp.float32)
    for k in range(lists):
        block = packed[k * most : (k + 1) * most].astype(jnp.int32).astype(jnp.int16)
        for ring in range(rings):
            out_ref[k, ring] = block


def merge_kernel(near_ref, after_ref, out_ref):
    del after_ref
    parents = out_ref.shape[0]
    first = lax.axis_index("lists") * parents
    width = out_ref.shape[1] - LANES
    near = near_ref[...].astype(jnp.int32)
    bits = (near[:, :LANES] & 1).astype(jnp.float32).astype(jnp.bfloat16)
    shape = (LANES, LANES)
    line, lane = lax.broadcasted_iota(jnp.int32, shape, 0), lax.broadcasted_iota(jnp.int32, shape, 1)
    values = jnp.zeros(shape, jnp.float32)
    start = 0
    for k, length in enumerate((SIZE_BITS, PARENT_BITS, EXPONENT_BITS)):
        keep = (lane == k) & (line >= start) & (line < start + length)
        value = (1 << jnp.minimum(jnp.maximum(line - start, 0), length)).astype(jnp.float32)
        values = jnp.where(keep, value, values)
        start += length
    note = jnp.dot(bits, values.astype(jnp.bfloat16), preferred_element_type=jnp.float32)
    size, parent, exponent = note[:, 0:1], note[:, 1:2], note[:, 2:3] - 128.0
    wanted = (lax.broadcasted_iota(jnp.int32, (near.shape[0], parents), 1) + first).astype(jnp.float32)
    pick = jnp.where(parent == wanted, 1.0, 0.0).astype(jnp.bfloat16)
    value = near.astype(jnp.float32) * (size * power(exponent - FRACTION))
    upper = value.astype(jnp.bfloat16)
    lower = (value - upper.astype(jnp.float32)).astype(jnp.bfloat16)

    def picked(rows):
        return lax.dot_general(pick, rows, (((0,), (0,)), ((), ())), preferred_element_type=jnp.float32)

    out_ref[:, :width] = picked(upper) + picked(lower)
    lane = lax.broadcasted_iota(jnp.int32, note.shape, 1)
    out_ref[:, width:] = picked(jnp.where(lane == 0, size, 0.0).astype(jnp.bfloat16))


def rotate_kernel(points_hbm, rotation_hbm, out_hbm, turned_hbm, points_ref, rotation_ref, out_ref, turned_ref, in_sems, out_sems):
    width, count = out_ref.shape
    piece, rows = count // PIECES, width // BLOCKS
    fetch = pltpu.make_async_copy(rotation_hbm, rotation_ref, in_sems.at[PIECES])
    fetch.start()
    parts = [slice(step * piece, (step + 1) * piece) for step in range(PIECES)]
    blocks = [slice(step * rows, (step + 1) * rows) for step in range(BLOCKS)]
    fetches = [
        pltpu.make_async_copy(points_hbm.at[part], points_ref.at[part], in_sems.at[k]) for k, part in enumerate(parts)
    ]
    for copy in fetches:
        copy.start()
    fetch.wait()
    turned_ref[...] = rotation_ref[...].T
    stores = [pltpu.make_async_copy(turned_ref, turned_hbm, out_sems.at[PIECES * BLOCKS])]
    stores[0].start()
    for k, part in enumerate(parts):
        fetches[k].wait()
        for j, block in enumerate(blocks):
            out_ref[block, part] = dot_nt(turned_ref[block, :], points_ref[part, :])
            store = pltpu.make_async_copy(
                out_ref.at[block, part], out_hbm.at[0, block, part], out_sems.at[k * BLOCKS + j]
            )
            store.start()
            stores.append(store)
    for store in stores:
        store.wait()


def code_kernel(
    whole_ref, turned_hbm, rotated_hbm, assign_ref, codes_ref,
    out_ref, merged_ref, all_ref, rot_ref, pick_ref, turned_ref, sems,
):
    width, count = rot_ref.shape
    parents = all_ref.shape[0]
    sub_width = width // codes_ref.shape[0]
    steps = codes_ref.shape[0] // (SIDE * UNROLL)
    rows = width // steps
    fetch = pltpu.make_async_copy(turned_hbm, turned_ref, sems.at[steps])
    fetch.start()

    def fetched(step):
        span = pl.ds(pl.multiple_of(step * rows, rows), rows)
        return pltpu.make_async_copy(rotated_hbm.at[0, span], rot_ref.at[span], sems.at[step])

    for step in range(steps):
        fetched(step).start()
    all_ref[...] = whole_ref[:, :width] / whole_ref[:, width : width + 1]
    shard_rows = merged_ref.shape[0]
    shard = lax.axis_index("z") * 2 + lax.axis_index("core")
    merged_ref[...] = all_ref[pl.ds(pl.multiple_of(shard * shard_rows, shard_rows), shard_rows), :]
    lowered = all_ref[...].astype(jnp.bfloat16)
    ids = lax.broadcasted_iota(jnp.int32, (parents, count), 0)
    pick = jnp.where(ids == assign_ref[...], 1.0, 0.0).astype(jnp.bfloat16)
    pick_ref[:parents, :] = pick
    pick_ref[parents:, :] = pick
    piece = count // PIECES

    def correct(step):
        span = pl.ds(pl.multiple_of(step * rows, rows), rows)
        parent = dot_nt(turned_ref[span, :], lowered)
        upper = parent.astype(jnp.bfloat16)
        lower = (parent - upper.astype(jnp.float32)).astype(jnp.bfloat16)
        both = jnp.concatenate([upper, lower], axis=1)
        fetched(step).wait()
        for k in range(PIECES):
            part = slice(k * piece, (k + 1) * piece)
            chosen = jnp.dot(both, pick_ref[:, part], preferred_element_type=jnp.float32)
            rot_ref[span, part] = rot_ref[span, part] - chosen

    def small(ids):
        return ids.astype(jnp.float32).astype(jnp.bfloat16)

    tile = 2 * sub_width
    low_ids = [small(lax.broadcasted_iota(jnp.int32, (tile, count), 0) + start) for start in range(0, LOW, tile)]
    pair_ids = small(lax.broadcasted_iota(jnp.int32, (tile, count), 0) // sub_width)
    high_ids = small(lax.broadcasted_iota(jnp.int32, (tile, count), 0) % HIGH)
    first_half = lax.broadcasted_iota(jnp.int32, (tile, count), 0) < HIGH
    spot = lax.broadcasted_iota(jnp.int32, (8, LANES), 1) // LOW
    line = lax.broadcasted_iota(jnp.int32, (8, LANES), 0)
    wide_line = lax.broadcasted_iota(jnp.int32, (8, CODEWORDS), 0)
    one, zero = jnp.ones((), jnp.bfloat16), jnp.zeros((), jnp.bfloat16)
    spots = LANES // LOW

    def part(rows, sub, place):
        rows = rows[:, sub // spots * LANES : (sub // spots + 1) * LANES]
        turn = (place - sub) % spots * LOW
        return pltpu.roll(rows, turn, 1) if turn else rows

    def spread(base):
        weights, masked, highs = [], [], []
        for sub in range(SIDE):
            index = base + sub
            code = codes_ref[pl.ds(index, 1), :]
            low = small(jnp.broadcast_to(code & (LOW - 1), (tile, count)))
            weights += [jnp.where(ids == low, one, zero) for ids in low_ids]
            value = rot_ref[pl.ds(pl.multiple_of(index * sub_width, sub_width), sub_width), :]
            value = jnp.concatenate([value, value], axis=0).astype(jnp.bfloat16)
            high = jnp.broadcast_to(code // LOW, (tile, count))
            highs.append(high)
            behind = small(high) - pair_ids
            for k in range(0, HIGH, 2):
                masked.append(jnp.where(behind == jnp.asarray(k, jnp.bfloat16), value, zero))
        for sub in range(0, SIDE, 2):
            high = small(jnp.where(first_half, highs[sub], highs[sub + 1]))
            masked.append(jnp.where(high_ids == high, one, zero))
        result = dot_nt(jnp.concatenate(masked, axis=0), jnp.concatenate(weights, axis=0))
        sums, counts = [], []
        for sub in range(SIDE):
            start = sub * HIGH * sub_width
            tally = result[SIDE * HIGH * sub_width + sub * HIGH :][:HIGH]
            halves, tallies = [], []
            for first in range(0, HIGH, spots):
                total, counted = None, None
                for k in range(first, first + spots):
                    piece = part(result[start + k * sub_width :][:sub_width], sub, k)
                    total = piece if total is None else jnp.where(spot == k % spots, piece, total)
                    piece = jnp.where(line == k, part(tally, sub, k), 0.0)
                    counted = piece if counted is None else jnp.where(spot == k % spots, piece, counted)
                halves.append(total)
                tallies.append(jnp.sum(counted, axis=0, keepdims=True))
            sums.append(halves)
            counts.append(tallies)
        return sums, counts

    fetch.wait()
    correct(0)
    for step in range(steps):
        if step + 1 < steps:
            correct(step + 1)
        sums, counts = [], []
        for k in range(UNROLL):
            more_sums, more_counts = spread((step * UNROLL + k) * SIDE)
            sums += more_sums
            counts += more_counts
        for k in range(SIDE * UNROLL // GROUP):
            mine = range(k * GROUP, (k + 1) * GROUP)
            lines = [jnp.concatenate(sums[sub], axis=1) for sub in mine]
            tally = jnp.zeros((8, CODEWORDS), jnp.float32)
            for place, sub in enumerate(mine):
                row = jnp.broadcast_to(jnp.concatenate(counts[sub], axis=1), (8, CODEWORDS))
                tally = jnp.where(wide_line == place, row, tally)
            out_ref[step * (SIDE * UNROLL // GROUP) + k] = jnp.concatenate(lines + [tally], axis=0)


def whole(count):
    return [pl.BlockSpec(memory_space=pltpu.VMEM)] * count


def anywhere(count):
    return [pl.BlockSpec(memory_space=pl.ANY)] * count


def shaped(shape, kind=jnp.float32):
    return jax.ShapeDtypeStruct(shape, kind)


def body(child_centroids, child_sizes, parent_of, points, assign, codes, rotation):
    lists, rings = lax.axis_size("lists"), lax.axis_size("z")
    chips = lists * rings
    core = lax.axis_index("core")
    child_count, width = child_centroids.shape
    count, subspaces = codes.shape
    owner_parents = rings * child_count
    shard_rows = child_count // 2
    most = child_count // math.isqrt(lists)
    wide = width + LANES

    packed = pl.pallas_call(
        functools.partial(pack_kernel, owner_parents),
        out_shape=shaped((lists, rings, most, width), jnp.int16),
        in_specs=anywhere(3),
        out_specs=whole(1)[0],
        scratch_shapes=[
            pltpu.VMEM((child_count, width), jnp.float32),
            pltpu.VMEM((1, child_count), jnp.int32),
            pltpu.VMEM((1, child_count), jnp.int32),
            pltpu.SemaphoreType.DMA((3,)),
        ],
        compiler_params=pltpu.CompilerParams(vmem_limit_bytes=FULL),
    )(child_centroids, child_sizes[None, :], parent_of[None, :])
    near = lax.all_to_all(packed.reshape(chips, most, width), ("lists", "z"), 0, 0)
    rotated, turned = pl.pallas_call(
        rotate_kernel,
        out_shape=(shaped((SLABS, width, count)), shaped((width, width), jnp.bfloat16)),
        in_specs=anywhere(2),
        out_specs=tuple(anywhere(2)),
        scratch_shapes=[
            pltpu.VMEM((count, width), jnp.bfloat16),
            pltpu.VMEM((width, width), jnp.bfloat16),
            pltpu.VMEM((width, count), jnp.float32),
            pltpu.VMEM((width, width), jnp.bfloat16),
            pltpu.SemaphoreType.DMA((PIECES + 1,)),
            pltpu.SemaphoreType.DMA((PIECES * BLOCKS + 1,)),
        ],
        compiler_params=pltpu.CompilerParams(vmem_limit_bytes=MOST),
        cost_estimate=pl.CostEstimate(flops=2 * width * width * count, bytes_accessed=10 << 20, transcendentals=0),
    )(points, rotation)
    mine = pl.pallas_call(
        merge_kernel,
        out_shape=shaped((owner_parents, wide)),
        in_specs=whole(1) + anywhere(1),
        out_specs=whole(1)[0],
        compiler_params=pltpu.CompilerParams(vmem_limit_bytes=SOME),
    )(near.reshape(chips * most, width), rotated)
    sums_of_list = mine + lax.ppermute(mine, "core", SWAP)
    groups = subspaces // GROUP
    rows = GROUP * (width // subspaces) + 8
    sums, merged = pl.pallas_call(
        code_kernel,
        out_shape=(shaped((groups, rows, CODEWORDS)), shaped((shard_rows, width))),
        in_specs=whole(1) + anywhere(2) + whole(2),
        out_specs=tuple(whole(2)),
        scratch_shapes=[
            pltpu.VMEM((owner_parents, width), jnp.float32),
            pltpu.VMEM((width, count), jnp.float32),
            pltpu.VMEM((2 * owner_parents, count), jnp.bfloat16),
            pltpu.VMEM((width, width), jnp.bfloat16),
            pltpu.SemaphoreType.DMA((subspaces // (SIDE * UNROLL) + 1,)),
        ],
        compiler_params=pltpu.CompilerParams(vmem_limit_bytes=SOME),
    )(sums_of_list, turned, rotated, assign[None, :], codes.T)

    half_groups = groups // 2
    splits = chips // half_groups
    sums = sums.reshape(2, half_groups, rows, splits, CODEWORDS // splits)
    sums = sums.transpose(0, 1, 3, 2, 4).reshape(2, chips, rows, CODEWORDS // splits)
    kept = lax.dynamic_index_in_dim(sums, core, 0, keepdims=False)
    given = lax.dynamic_index_in_dim(sums, 1 - core, 0, keepdims=False)
    taken = lax.ppermute(given, "core", SWAP)
    chip = (kept.astype(jnp.float32) + taken.astype(jnp.float32)).astype(jnp.bfloat16)
    total = jnp.sum(lax.all_to_all(chip, ("lists", "z"), 0, 0).astype(jnp.float32), axis=0)
    sub_width = (rows - 8) // GROUP
    tops = total[: rows - 8].reshape(GROUP, sub_width, -1)
    means = tops / (1.0 + total[rows - 8 : rows - 8 + GROUP, None, :])
    means = means.reshape(1, rows - 8, -1).astype(jnp.bfloat16)
    means = jnp.broadcast_to(means, (chips,) + means.shape[1:])
    mine = lax.all_to_all(means, ("lists", "z"), 0, 0)
    mine = mine.reshape(half_groups, splits, rows - 8, -1).transpose(0, 2, 1, 3).reshape(-1, CODEWORDS)
    other = lax.ppermute(mine, "core", SWAP)
    first = core == 0
    means = jnp.concatenate([jnp.where(first, mine, other), jnp.where(first, other, mine)], axis=0)
    return merged, means.astype(jnp.float32)


def solution(mesh):
    lists, points = mesh.devices.shape
    split = jax.sharding.Mesh(mesh.devices.reshape(lists, points // 2, 2), ("lists", "z", "core"))
    every = ("lists", "z", "core")
    in_specs = (P(every, None), P(every), P(every), P(every, None), P(every), P(every, None), P())
    out_specs = (P(every, None), P())
    return jax.shard_map(body, mesh=split, in_specs=in_specs, out_specs=out_specs, check_vma=False)
```

```python
import functools
import math

import jax
import jax.numpy as jnp
from jax import lax
from jax.experimental import pallas as pl
from jax.experimental.pallas import tpu as pltpu
from jax.sharding import PartitionSpec as P

CODEWORDS = 256
LOW = 32
HIGH = CODEWORDS // LOW
GROUP = 3
SIDE = 8
UNROLL = 3
FRACTION = 14.0
SIZE_BITS, PARENT_BITS, EXPONENT_BITS = 9, 13, 8
SLABS = 4
PIECES = 3
LANES = 128

FULL = 66_900_000
MOST = 66_200_000
SOME = 50_000_000
SWAP = ((0, 1), (1, 0))


def dot_nt(a, b):
    return lax.dot_general(a, b, (((1,), (1,)), ((), ())), preferred_element_type=jnp.float32)


def as_column(row):
    count = row.shape[1]
    shape = (count, count)
    here = lax.broadcasted_iota(jnp.int32, shape, 0) == lax.broadcasted_iota(jnp.int32, shape, 1)
    return jnp.sum(jnp.where(here, jnp.broadcast_to(row, shape), 0), axis=1, keepdims=True)


def power(exponent):
    return jnp.exp2(exponent)


def pack_kernel(owner_parents, child_hbm, size_hbm, parent_hbm, out_ref, child_ref, size_ref, parent_ref, sems):
    copies = [
        pltpu.make_async_copy(source, target, sems.at[k])
        for k, (source, target) in enumerate(
            ((child_hbm, child_ref), (size_hbm, size_ref), (parent_hbm, parent_ref))
        )
    ]
    for copy in copies:
        copy.start()
    for copy in copies:
        copy.wait()
    lists, rings, most, width = out_ref.shape
    count = child_ref.shape[0]
    parent_row = parent_ref[...]
    parent = as_column(parent_row)
    size = as_column(size_ref[...])
    owner_row, owner = parent_row // owner_parents, parent // owner_parents
    shape = (count, count)
    before = lax.broadcasted_iota(jnp.int32, shape, 0) < lax.broadcasted_iota(jnp.int32, shape, 1)
    earlier = jnp.where((owner == owner_row) & before, 1, 0)
    slot = owner_row * most + jnp.sum(earlier, axis=0, keepdims=True)
    slots = lax.broadcasted_iota(jnp.int32, (lists * most, count), 0)
    pack = jnp.where(slots == slot, 1.0, 0.0).astype(jnp.bfloat16)
    child = child_ref[...]
    top = jnp.max(jnp.abs(child), axis=1, keepdims=True)
    exponent = jnp.ceil(jnp.log2(jnp.maximum(top, 1e-30)))
    scaled = jnp.floor(child * power(FRACTION - exponent) + 0.5)
    word = size + (parent << SIZE_BITS)
    word = word + ((exponent.astype(jnp.int32) + 128) << (SIZE_BITS + PARENT_BITS))
    lane = lax.broadcasted_iota(jnp.int32, (count, LANES), 1)
    bit = (jnp.broadcast_to(word, (count, LANES)) >> jnp.minimum(lane, 31)) & 1
    marked = 2.0 * jnp.floor(scaled[:, :LANES] * 0.5) + bit.astype(jnp.float32)
    sent = jnp.concatenate([marked, scaled[:, LANES:]], axis=1)
    upper = jnp.floor(sent * (1.0 / 128.0))
    lower = sent - upper * 128.0
    packed = 128.0 * jnp.dot(pack, upper.astype(jnp.bfloat16), preferred_element_type=jnp.float32)
    packed = packed + jnp.dot(pack, lower.astype(jnp.bfloat16), preferred_element_type=jnp.float32)
    for k in range(lists):
        block = packed[k * most : (k + 1) * most].astype(jnp.int32).astype(jnp.int16)
        for ring in range(rings):
            out_ref[k, ring] = block


def merge_kernel(near_ref, after_ref, out_ref):
    del after_ref
    parents = out_ref.shape[0]
    first = lax.axis_index("lists") * parents
    width = out_ref.shape[1] - LANES
    near = near_ref[...].astype(jnp.int32)
    bits = (near[:, :LANES] & 1).astype(jnp.float32).astype(jnp.bfloat16)
    shape = (LANES, LANES)
    line, lane = lax.broadcasted_iota(jnp.int32, shape, 0), lax.broadcasted_iota(jnp.int32, shape, 1)
    values = jnp.zeros(shape, jnp.float32)
    start = 0
    for k, length in enumerate((SIZE_BITS, PARENT_BITS, EXPONENT_BITS)):
        keep = (lane == k) & (line >= start) & (line < start + length)
        value = (1 << jnp.minimum(jnp.maximum(line - start, 0), length)).astype(jnp.float32)
        values = jnp.where(keep, value, values)
        start += length
    note = jnp.dot(bits, values.astype(jnp.bfloat16), preferred_element_type=jnp.float32)
    size, parent, exponent = note[:, 0:1], note[:, 1:2], note[:, 2:3] - 128.0
    wanted = (lax.broadcasted_iota(jnp.int32, (near.shape[0], parents), 1) + first).astype(jnp.float32)
    pick = jnp.where(parent == wanted, 1.0, 0.0).astype(jnp.bfloat16)
    value = near.astype(jnp.float32) * (size * power(exponent - FRACTION))
    upper = value.astype(jnp.bfloat16)
    lower = (value - upper.astype(jnp.float32)).astype(jnp.bfloat16)

    def picked(rows):
        return lax.dot_general(pick, rows, (((0,), (0,)), ((), ())), preferred_element_type=jnp.float32)

    out_ref[:, :width] = picked(upper) + picked(lower)
    lane = lax.broadcasted_iota(jnp.int32, note.shape, 1)
    out_ref[:, width:] = picked(jnp.where(lane == 0, size, 0.0).astype(jnp.bfloat16))


def rotate_kernel(
    points_hbm, points_other_hbm, codes_hbm, codes_other_hbm, assign_hbm, assign_other_hbm, rotation_hbm,
    out_hbm, turned_hbm,
    points_ref, codes_ref, assign_ref, rotation_ref, out_ref, turned_ref, note_ref, in_sems, out_sems,
):
    width, count = out_ref.shape
    own = count // 2
    subspaces = codes_ref.shape[1] // 2
    piece = own // PIECES
    core = lax.axis_index("core")
    first = pl.multiple_of(core * width, LANES)
    fetch = pltpu.make_async_copy(rotation_hbm, rotation_ref, in_sems.at[0])
    fetch.start()
    fetches = []
    for side, source in enumerate((points_hbm, points_other_hbm)):
        for k in range(PIECES):
            part = slice(k * piece, (k + 1) * piece)
            target = points_ref.at[side * own + k * piece : side * own + (k + 1) * piece]
            fetches.append(pltpu.make_async_copy(source.at[part], target, in_sems.at[1 + side * PIECES + k]))
    notes = []
    for k, (source, target) in enumerate(
        (
            (codes_hbm, codes_ref.at[0]),
            (codes_other_hbm, codes_ref.at[1]),
            (assign_hbm, assign_ref.at[0]),
            (assign_other_hbm, assign_ref.at[1]),
        )
    ):
        notes.append(pltpu.make_async_copy(source, target, in_sems.at[1 + 2 * PIECES + k]))
    for copy in fetches + notes:
        copy.start()
    fetch.wait()
    turned_ref[...] = rotation_ref[:, pl.ds(first, width)].T
    stores = [pltpu.make_async_copy(turned_ref, turned_hbm, out_sems.at[2 * PIECES])]
    stores[0].start()
    for k in range(2 * PIECES):
        part = slice(k * piece, (k + 1) * piece)
        fetches[k].wait()
        out_ref[:, part] = dot_nt(turned_ref[...], points_ref[part, :])
        store = pltpu.make_async_copy(out_ref.at[:, part], out_hbm.at[0, :, part], out_sems.at[k])
        store.start()
        stores.append(store)
    for copy in notes:
        copy.wait()
    chosen = pl.ds(pl.multiple_of(core * subspaces, 8), subspaces)
    for side in range(2):
        part = slice(side * own, (side + 1) * own)
        code = codes_ref[side, chosen, :]
        note_ref[:subspaces, part] = (code & (LOW - 1)).astype(jnp.float32)
        note_ref[subspaces : 2 * subspaces, part] = (code // LOW).astype(jnp.float32)
        note_ref[2 * subspaces :, part] = jnp.broadcast_to(assign_ref[side].astype(jnp.float32), (8, own))
    store = pltpu.make_async_copy(note_ref, out_hbm.at[1, : 2 * subspaces + 8], out_sems.at[2 * PIECES + 1])
    store.start()
    stores.append(store)
    for store in stores:
        store.wait()


def code_kernel(
    whole_ref, turned_hbm, rotated_hbm, out_ref, merged_ref, all_ref, rot_ref, pick_ref, turned_ref, note_ref, sems
):
    width, count = rot_ref.shape
    parents, columns = all_ref.shape
    subspaces = out_ref.shape[0] * GROUP
    sub_width = width // subspaces
    steps = subspaces // (SIDE * UNROLL)
    rows = width // steps
    note = pltpu.make_async_copy(rotated_hbm.at[1, : 2 * subspaces + 8], note_ref, sems.at[steps + 1])
    note.start()
    fetch = pltpu.make_async_copy(turned_hbm, turned_ref, sems.at[steps])
    fetch.start()

    def fetched(step):
        span = pl.ds(step * rows, rows)
        return pltpu.make_async_copy(rotated_hbm.at[0, span], rot_ref.at[span], sems.at[step])

    for step in range(steps):
        fetched(step).start()
    all_ref[...] = whole_ref[:, :columns] / whole_ref[:, columns : columns + 1]
    shard_rows = merged_ref.shape[0]
    shard = lax.axis_index("z") * 2 + lax.axis_index("core")
    merged_ref[...] = all_ref[pl.ds(pl.multiple_of(shard * shard_rows, shard_rows), shard_rows), :]
    lowered = all_ref[...].astype(jnp.bfloat16)
    note.wait()
    ids = lax.broadcasted_iota(jnp.int32, (parents, count), 0).astype(jnp.float32)
    pick = jnp.where(ids == note_ref[2 * subspaces : 2 * subspaces + 1, :], 1.0, 0.0).astype(jnp.bfloat16)
    pick_ref[:parents, :] = pick
    pick_ref[parents:, :] = pick
    piece = count // (2 * PIECES)

    def correct(step):
        span = pl.ds(step * rows, rows)
        parent = dot_nt(turned_ref[span, :], lowered)
        upper = parent.astype(jnp.bfloat16)
        lower = (parent - upper.astype(jnp.float32)).astype(jnp.bfloat16)
        both = jnp.concatenate([upper, lower], axis=1)
        fetched(step).wait()
        for k in range(2 * PIECES):
            part = slice(k * piece, (k + 1) * piece)
            chosen = jnp.dot(both, pick_ref[:, part], preferred_element_type=jnp.float32)
            rot_ref[span, part] = rot_ref[span, part] - chosen

    def small(ids):
        return ids.astype(jnp.float32).astype(jnp.bfloat16)

    tile = 2 * sub_width
    low_ids = [small(lax.broadcasted_iota(jnp.int32, (tile, count), 0) + start) for start in range(0, LOW, tile)]
    pair_ids = small(lax.broadcasted_iota(jnp.int32, (tile, count), 0) // sub_width)
    high_ids = small(lax.broadcasted_iota(jnp.int32, (tile, count), 0) % HIGH)
    first_half = lax.broadcasted_iota(jnp.int32, (tile, count), 0) < HIGH
    spot = lax.broadcasted_iota(jnp.int32, (8, LANES), 1) // LOW
    line = lax.broadcasted_iota(jnp.int32, (8, LANES), 0)
    wide_line = lax.broadcasted_iota(jnp.int32, (8, CODEWORDS), 0)
    one, zero = jnp.ones((), jnp.bfloat16), jnp.zeros((), jnp.bfloat16)
    spots = LANES // LOW

    def part(rows, sub, place):
        rows = rows[:, sub // spots * LANES : (sub // spots + 1) * LANES]
        turn = (place - sub) % spots * LOW
        return pltpu.roll(rows, turn, 1) if turn else rows

    def spread(base):
        weights, masked, highs = [], [], []
        for sub in range(SIDE):
            index = base + sub
            low = jnp.broadcast_to(note_ref[index : index + 1, :], (tile, count)).astype(jnp.bfloat16)
            weights += [jnp.where(ids == low, one, zero) for ids in low_ids]
            value = rot_ref[index * sub_width : (index + 1) * sub_width, :]
            value = jnp.concatenate([value, value], axis=0).astype(jnp.bfloat16)
            high = jnp.broadcast_to(note_ref[subspaces + index : subspaces + index + 1, :], (tile, count))
            highs.append(high)
            behind = high.astype(jnp.bfloat16) - pair_ids
            for k in range(0, HIGH, 2):
                masked.append(jnp.where(behind == jnp.asarray(k, jnp.bfloat16), value, zero))
        for sub in range(0, SIDE, 2):
            high = jnp.where(first_half, highs[sub], highs[sub + 1]).astype(jnp.bfloat16)
            masked.append(jnp.where(high_ids == high, one, zero))
        result = dot_nt(jnp.concatenate(masked, axis=0), jnp.concatenate(weights, axis=0))
        sums, counts = [], []
        for sub in range(SIDE):
            start = sub * HIGH * sub_width
            tally = result[SIDE * HIGH * sub_width + sub * HIGH :][:HIGH]
            halves, tallies = [], []
            for first in range(0, HIGH, spots):
                total, counted = None, None
                for k in range(first, first + spots):
                    piece = part(result[start + k * sub_width :][:sub_width], sub, k)
                    total = piece if total is None else jnp.where(spot == k % spots, piece, total)
                    piece = jnp.where(line == k, part(tally, sub, k), 0.0)
                    counted = piece if counted is None else jnp.where(spot == k % spots, piece, counted)
                halves.append(total)
                tallies.append(jnp.sum(counted, axis=0, keepdims=True))
            sums.append(halves)
            counts.append(tallies)
        return sums, counts

    fetch.wait()
    correct(0)
    for step in range(steps):
        if step + 1 < steps:
            correct(step + 1)
        sums, counts = [], []
        for k in range(UNROLL):
            more_sums, more_counts = spread((step * UNROLL + k) * SIDE)
            sums += more_sums
            counts += more_counts
        for k in range(SIDE * UNROLL // GROUP):
            mine = range(k * GROUP, (k + 1) * GROUP)
            lines = [jnp.concatenate(sums[sub], axis=1) for sub in mine]
            tally = jnp.zeros((8, CODEWORDS), jnp.float32)
            for place, sub in enumerate(mine):
                row = jnp.broadcast_to(jnp.concatenate(counts[sub], axis=1), (8, CODEWORDS))
                tally = jnp.where(wide_line == place, row, tally)
            out_ref[step * (SIDE * UNROLL // GROUP) + k] = jnp.concatenate(lines + [tally], axis=0).astype(jnp.bfloat16)


def whole(count):
    return [pl.BlockSpec(memory_space=pltpu.VMEM)] * count


def anywhere(count):
    return [pl.BlockSpec(memory_space=pl.ANY)] * count


def shaped(shape, kind=jnp.float32):
    return jax.ShapeDtypeStruct(shape, kind)


def body(child_centroids, child_sizes, parent_of, points, assign, codes, rotation):
    lists, rings = lax.axis_size("lists"), lax.axis_size("z")
    chips = lists * rings
    core = lax.axis_index("core")
    child_count, width = child_centroids.shape
    count, subspaces = codes.shape
    owner_parents = rings * child_count
    shard_rows = child_count // 2
    most = child_count // math.isqrt(lists)
    wide = width + LANES

    packed = pl.pallas_call(
        functools.partial(pack_kernel, owner_parents),
        out_shape=shaped((lists, rings, most, width), jnp.int16),
        in_specs=anywhere(3),
        out_specs=whole(1)[0],
        scratch_shapes=[
            pltpu.VMEM((child_count, width), jnp.float32),
            pltpu.VMEM((1, child_count), jnp.int32),
            pltpu.VMEM((1, child_count), jnp.int32),
            pltpu.SemaphoreType.DMA((3,)),
        ],
        compiler_params=pltpu.CompilerParams(vmem_limit_bytes=FULL),
    )(child_centroids, child_sizes[None, :], parent_of[None, :])
    near = lax.all_to_all(packed.reshape(chips, most, width), ("lists", "z"), 0, 0)
    half_width, half_subspaces, pair_count = width // 2, subspaces // 2, 2 * count
    turned_codes, parent_row = codes.T, assign[None, :]

    def both(array):
        return array, lax.ppermute(array, "core", SWAP)

    rotated, turned = pl.pallas_call(
        rotate_kernel,
        out_shape=(shaped((SLABS, half_width, pair_count)), shaped((half_width, width), jnp.bfloat16)),
        in_specs=anywhere(7),
        out_specs=tuple(anywhere(2)),
        scratch_shapes=[
            pltpu.VMEM((pair_count, width), jnp.bfloat16),
            pltpu.VMEM((2, subspaces, count), jnp.int32),
            pltpu.VMEM((2, 1, count), jnp.int32),
            pltpu.VMEM((width, width), jnp.bfloat16),
            pltpu.VMEM((half_width, pair_count), jnp.float32),
            pltpu.VMEM((half_width, width), jnp.bfloat16),
            pltpu.VMEM((subspaces + 8, pair_count), jnp.float32),
            pltpu.SemaphoreType.DMA((2 * PIECES + 5,)),
            pltpu.SemaphoreType.DMA((2 * PIECES + 2,)),
        ],
        compiler_params=pltpu.CompilerParams(vmem_limit_bytes=MOST),
        cost_estimate=pl.CostEstimate(flops=2 * width * width * count, bytes_accessed=14 << 20, transcendentals=0),
    )(*both(points), *both(turned_codes), *both(parent_row), rotation)
    mine = pl.pallas_call(
        merge_kernel,
        out_shape=shaped((owner_parents, wide)),
        in_specs=whole(1) + anywhere(1),
        out_specs=whole(1)[0],
        compiler_params=pltpu.CompilerParams(vmem_limit_bytes=SOME),
    )(near.reshape(chips * most, width), rotated)
    sums_of_list = mine + lax.ppermute(mine, "core", SWAP)
    groups = half_subspaces // GROUP
    rows = GROUP * (width // subspaces) + 8
    sums, merged = pl.pallas_call(
        code_kernel,
        out_shape=(shaped((groups, rows, CODEWORDS), jnp.bfloat16), shaped((shard_rows, width))),
        in_specs=whole(1) + anywhere(2),
        out_specs=tuple(whole(2)),
        scratch_shapes=[
            pltpu.VMEM((owner_parents, width), jnp.float32),
            pltpu.VMEM((half_width, pair_count), jnp.float32),
            pltpu.VMEM((2 * owner_parents, pair_count), jnp.bfloat16),
            pltpu.VMEM((half_width, width), jnp.bfloat16),
            pltpu.VMEM((subspaces + 8, pair_count), jnp.float32),
            pltpu.SemaphoreType.DMA((half_subspaces // (SIDE * UNROLL) + 2,)),
        ],
        compiler_params=pltpu.CompilerParams(vmem_limit_bytes=SOME),
    )(sums_of_list, turned, rotated)

    splits = chips // groups
    chip = sums.reshape(groups, rows, splits, CODEWORDS // splits)
    chip = chip.transpose(0, 2, 1, 3).reshape(chips, rows, CODEWORDS // splits)
    total = jnp.sum(lax.all_to_all(chip, ("lists", "z"), 0, 0).astype(jnp.float32), axis=0)
    sub_width = (rows - 8) // GROUP
    tops = total[: rows - 8].reshape(GROUP, sub_width, -1)
    means = tops / (1.0 + total[rows - 8 : rows - 8 + GROUP, None, :])
    means = means.reshape(1, rows - 8, -1).astype(jnp.bfloat16)
    means = jnp.broadcast_to(means, (chips,) + means.shape[1:])
    mine = lax.all_to_all(means, ("lists", "z"), 0, 0)
    mine = mine.reshape(groups, splits, rows - 8, -1).transpose(0, 2, 1, 3).reshape(-1, CODEWORDS)
    other = lax.ppermute(mine, "core", SWAP)
    first = core == 0
    means = jnp.concatenate([jnp.where(first, mine, other), jnp.where(first, other, mine)], axis=0)
    return merged, means.astype(jnp.float32)


def solution(mesh):
    lists, points = mesh.devices.shape
    split = jax.sharding.Mesh(mesh.devices.reshape(lists, points // 2, 2), ("lists", "z", "core"))
    every = ("lists", "z", "core")
    in_specs = (P(every, None), P(every), P(every), P(every, None), P(every), P(every, None), P())
    out_specs = (P(every, None), P())
    return jax.shard_map(body, mesh=split, in_specs=in_specs, out_specs=out_specs, check_vma=False)
```

```python
import functools
import math

import jax
import jax.numpy as jnp
from jax import lax
from jax.experimental import pallas as pl
from jax.experimental.pallas import tpu as pltpu
from jax.sharding import PartitionSpec as P

CODEWORDS = 256
LOW = 32
HIGH = CODEWORDS // LOW
GROUP = 3
SIDE = 8
SHARES = (2, 4)
FRACTION = 14.0
SIZE_BITS, PARENT_BITS, EXPONENT_BITS = 9, 13, 8
SLABS = 4
PIECES = 3
LANES = 128

FULL = 66_900_000
MOST = 66_200_000
SOME = 50_000_000
SWAP = ((0, 1), (1, 0))


def dot_nt(a, b):
    return lax.dot_general(a, b, (((1,), (1,)), ((), ())), preferred_element_type=jnp.float32)


def as_column(row):
    count = row.shape[1]
    shape = (count, count)
    here = lax.broadcasted_iota(jnp.int32, shape, 0) == lax.broadcasted_iota(jnp.int32, shape, 1)
    return jnp.sum(jnp.where(here, jnp.broadcast_to(row, shape), 0), axis=1, keepdims=True)


def power(exponent):
    return jnp.exp2(exponent)


def pack_kernel(owner_parents, child_hbm, size_hbm, parent_hbm, out_ref, child_ref, size_ref, parent_ref, sems):
    copies = [
        pltpu.make_async_copy(source, target, sems.at[k])
        for k, (source, target) in enumerate(
            ((child_hbm, child_ref), (size_hbm, size_ref), (parent_hbm, parent_ref))
        )
    ]
    for copy in copies:
        copy.start()
    for copy in copies:
        copy.wait()
    lists, rings, most, width = out_ref.shape
    count = child_ref.shape[0]
    parent_row = parent_ref[...]
    parent = as_column(parent_row)
    size = as_column(size_ref[...])
    owner_row, owner = parent_row // owner_parents, parent // owner_parents
    shape = (count, count)
    before = lax.broadcasted_iota(jnp.int32, shape, 0) < lax.broadcasted_iota(jnp.int32, shape, 1)
    earlier = jnp.where((owner == owner_row) & before, 1, 0)
    slot = owner_row * most + jnp.sum(earlier, axis=0, keepdims=True)
    slots = lax.broadcasted_iota(jnp.int32, (lists * most, count), 0)
    pack = jnp.where(slots == slot, 1.0, 0.0).astype(jnp.bfloat16)
    child = child_ref[...]
    top = jnp.max(jnp.abs(child), axis=1, keepdims=True)
    exponent = jnp.ceil(jnp.log2(jnp.maximum(top, 1e-30)))
    scaled = jnp.floor(child * power(FRACTION - exponent) + 0.5)
    word = size + (parent << SIZE_BITS)
    word = word + ((exponent.astype(jnp.int32) + 128) << (SIZE_BITS + PARENT_BITS))
    lane = lax.broadcasted_iota(jnp.int32, (count, LANES), 1)
    bit = (jnp.broadcast_to(word, (count, LANES)) >> jnp.minimum(lane, 31)) & 1
    marked = 2.0 * jnp.floor(scaled[:, :LANES] * 0.5) + bit.astype(jnp.float32)
    sent = jnp.concatenate([marked, scaled[:, LANES:]], axis=1)
    upper = jnp.floor(sent * (1.0 / 128.0))
    lower = sent - upper * 128.0
    packed = 128.0 * jnp.dot(pack, upper.astype(jnp.bfloat16), preferred_element_type=jnp.float32)
    packed = packed + jnp.dot(pack, lower.astype(jnp.bfloat16), preferred_element_type=jnp.float32)
    for k in range(lists):
        block = packed[k * most : (k + 1) * most].astype(jnp.int32).astype(jnp.int16)
        for ring in range(rings):
            out_ref[k, ring] = block


def merge_kernel(near_ref, after_ref, out_ref):
    del after_ref
    parents = out_ref.shape[0]
    first = lax.axis_index("lists") * parents
    width = out_ref.shape[1] - LANES
    near = near_ref[...].astype(jnp.int32)
    bits = (near[:, :LANES] & 1).astype(jnp.float32).astype(jnp.bfloat16)
    shape = (LANES, LANES)
    line, lane = lax.broadcasted_iota(jnp.int32, shape, 0), lax.broadcasted_iota(jnp.int32, shape, 1)
    values = jnp.zeros(shape, jnp.float32)
    start = 0
    for k, length in enumerate((SIZE_BITS, PARENT_BITS, EXPONENT_BITS)):
        keep = (lane == k) & (line >= start) & (line < start + length)
        value = (1 << jnp.minimum(jnp.maximum(line - start, 0), length)).astype(jnp.float32)
        values = jnp.where(keep, value, values)
        start += length
    note = jnp.dot(bits, values.astype(jnp.bfloat16), preferred_element_type=jnp.float32)
    size, parent, exponent = note[:, 0:1], note[:, 1:2], note[:, 2:3] - 128.0
    wanted = (lax.broadcasted_iota(jnp.int32, (near.shape[0], parents), 1) + first).astype(jnp.float32)
    pick = jnp.where(parent == wanted, 1.0, 0.0).astype(jnp.bfloat16)
    value = near.astype(jnp.float32) * (size * power(exponent - FRACTION))
    upper = value.astype(jnp.bfloat16)
    lower = (value - upper.astype(jnp.float32)).astype(jnp.bfloat16)

    def picked(rows):
        return lax.dot_general(pick, rows, (((0,), (0,)), ((), ())), preferred_element_type=jnp.float32)

    out_ref[:, :width] = picked(upper) + picked(lower)
    lane = lax.broadcasted_iota(jnp.int32, note.shape, 1)
    out_ref[:, width:] = picked(jnp.where(lane == 0, size, 0.0).astype(jnp.bfloat16))


def rotate_kernel(
    points_hbm, points_other_hbm, codes_hbm, codes_other_hbm, assign_hbm, assign_other_hbm, rotation_hbm,
    out_hbm, early_hbm, turned_hbm,
    points_ref, codes_ref, assign_ref, rotation_ref, out_ref, turned_ref, note_ref, in_sems, out_sems,
):
    width, count = out_ref.shape
    own = count // 2
    subspaces = codes_ref.shape[1] // 2
    piece = own // PIECES
    core = lax.axis_index("core")
    first = pl.multiple_of(core * width, LANES)
    fetch = pltpu.make_async_copy(rotation_hbm, rotation_ref, in_sems.at[0])
    fetch.start()
    fetches = []
    for side, source in enumerate((points_hbm, points_other_hbm)):
        for k in range(PIECES):
            part = slice(k * piece, (k + 1) * piece)
            target = points_ref.at[side * own + k * piece : side * own + (k + 1) * piece]
            fetches.append(pltpu.make_async_copy(source.at[part], target, in_sems.at[1 + side * PIECES + k]))
    notes = []
    for k, (source, target) in enumerate(
        (
            (codes_hbm, codes_ref.at[0]),
            (codes_other_hbm, codes_ref.at[1]),
            (assign_hbm, assign_ref.at[0]),
            (assign_other_hbm, assign_ref.at[1]),
        )
    ):
        notes.append(pltpu.make_async_copy(source, target, in_sems.at[1 + 2 * PIECES + k]))
    for copy in fetches + notes:
        copy.start()
    fetch.wait()
    turned_ref[...] = rotation_ref[:, pl.ds(first, width)].T
    early = SHARES[0] * SIDE * (width // subspaces)
    stores = [pltpu.make_async_copy(turned_ref, turned_hbm, out_sems.at[4 * PIECES])]
    stores[0].start()
    for k in range(2 * PIECES):
        part = slice(k * piece, (k + 1) * piece)
        fetches[k].wait()
        out_ref[:, part] = dot_nt(turned_ref[...], points_ref[part, :])
        for j, (source, target) in enumerate(
            (
                (out_ref.at[:early, part], early_hbm.at[:early, part]),
                (out_ref.at[early:, part], out_hbm.at[0, early:, part]),
            )
        ):
            store = pltpu.make_async_copy(source, target, out_sems.at[2 * k + j])
            store.start()
            stores.append(store)
    for copy in notes:
        copy.wait()
    chosen = pl.ds(pl.multiple_of(core * subspaces, 8), subspaces)
    for side in range(2):
        part = slice(side * own, (side + 1) * own)
        code = codes_ref[side, chosen, :]
        low, high = (code & (LOW - 1)).astype(jnp.float32), (code // LOW).astype(jnp.float32)
        for start in range(0, subspaces, SIDE):
            note_ref[2 * start : 2 * start + SIDE, part] = low[start : start + SIDE]
            note_ref[2 * start + SIDE : 2 * (start + SIDE), part] = high[start : start + SIDE]
        note_ref[2 * subspaces :, part] = jnp.broadcast_to(assign_ref[side].astype(jnp.float32), (8, own))
    lines, after = 2 * SHARES[0] * SIDE, 2 * subspaces
    for k, (source, target) in enumerate(
        (
            (note_ref.at[:lines], early_hbm.at[early : early + lines]),
            (note_ref.at[after:], early_hbm.at[early + lines :]),
            (note_ref.at[lines:after], out_hbm.at[1, lines:after]),
        )
    ):
        store = pltpu.make_async_copy(source, target, out_sems.at[4 * PIECES + 1 + k])
        store.start()
        stores.append(store)
    for store in stores:
        store.wait()


def code_kernel(
    whole_ref, early_ref, turned_ref, rotated_hbm, out_ref, merged_hbm, all_ref, rot_ref, pick_ref, note_ref, sems
):
    width, count = rot_ref.shape
    parents, columns = all_ref.shape
    subspaces = out_ref.shape[0] * GROUP
    sub_width = width // subspaces
    shares = len(SHARES)
    ends = [sum(SHARES[: k + 1]) * SIDE for k in range(shares)]
    starts = [0] + ends[:-1]
    early = ends[0] * sub_width

    def columns_of(share):
        return slice(starts[share] * sub_width, ends[share] * sub_width)

    fetches, notes = [None], [None]
    for share in range(1, shares):
        span = columns_of(share)
        fetches.append(pltpu.make_async_copy(rotated_hbm.at[0, span], rot_ref.at[span], sems.at[share]))
        span = slice(2 * starts[share], 2 * ends[share])
        notes.append(pltpu.make_async_copy(rotated_hbm.at[1, span], note_ref.at[span], sems.at[shares + share]))
        fetches[share].start()
        notes[share].start()
    all_ref[...] = whole_ref[:, :columns] / whole_ref[:, columns : columns + 1]
    shard_rows = merged_hbm.shape[0]
    shard = lax.axis_index("z") * 2 + lax.axis_index("core")
    mine = all_ref.at[pl.ds(pl.multiple_of(shard * shard_rows, shard_rows), shard_rows)]
    store = pltpu.make_async_copy(mine, merged_hbm, sems.at[0])
    store.start()
    lowered = all_ref[...].astype(jnp.bfloat16)
    ids = lax.broadcasted_iota(jnp.int32, (parents, count), 0).astype(jnp.float32)
    pick = jnp.where(ids == early_ref[early + 2 * ends[0] : early + 2 * ends[0] + 1, :], 1.0, 0.0).astype(jnp.bfloat16)
    pick_ref[:parents, :] = pick
    pick_ref[parents:, :] = pick
    piece = count // (2 * PIECES)

    def correct(share):
        span = columns_of(share)
        parent = dot_nt(turned_ref[span, :], lowered)
        upper = parent.astype(jnp.bfloat16)
        lower = (parent - upper.astype(jnp.float32)).astype(jnp.bfloat16)
        both = jnp.concatenate([upper, lower], axis=1)
        if share:
            fetches[share].wait()
        source = rot_ref if share else early_ref
        for k in range(2 * PIECES):
            part = slice(k * piece, (k + 1) * piece)
            chosen = jnp.dot(both, pick_ref[:, part], preferred_element_type=jnp.float32)
            rot_ref[span, part] = source[span, part] - chosen

    def small(ids):
        return ids.astype(jnp.float32).astype(jnp.bfloat16)

    tile = 2 * sub_width
    low_ids = [small(lax.broadcasted_iota(jnp.int32, (tile, count), 0) + start) for start in range(0, LOW, tile)]
    pair_ids = small(lax.broadcasted_iota(jnp.int32, (tile, count), 0) // sub_width)
    high_ids = small(lax.broadcasted_iota(jnp.int32, (tile, count), 0) % HIGH)
    first_half = lax.broadcasted_iota(jnp.int32, (tile, count), 0) < HIGH
    spot = lax.broadcasted_iota(jnp.int32, (8, LANES), 1) // LOW
    line = lax.broadcasted_iota(jnp.int32, (8, LANES), 0)
    wide_line = lax.broadcasted_iota(jnp.int32, (8, CODEWORDS), 0)
    one, zero = jnp.ones((), jnp.bfloat16), jnp.zeros((), jnp.bfloat16)
    spots = LANES // LOW

    def part(rows, sub, place):
        rows = rows[:, sub // spots * LANES : (sub // spots + 1) * LANES]
        turn = (place - sub) % spots * LOW
        return pltpu.roll(rows, turn, 1) if turn else rows

    def spread(base):
        weights, masked, highs = [], [], []
        note = note_ref if base >= ends[0] else early_ref.at[early:]
        for sub in range(SIDE):
            index = base + sub
            low = jnp.broadcast_to(note[2 * base + sub : 2 * base + sub + 1, :], (tile, count)).astype(jnp.bfloat16)
            weights += [jnp.where(ids == low, one, zero) for ids in low_ids]
            value = rot_ref[index * sub_width : (index + 1) * sub_width, :]
            value = jnp.concatenate([value, value], axis=0).astype(jnp.bfloat16)
            high = jnp.broadcast_to(note[2 * base + SIDE + sub : 2 * base + SIDE + sub + 1, :], (tile, count))
            highs.append(high)
            behind = high.astype(jnp.bfloat16) - pair_ids
            for k in range(0, HIGH, 2):
                masked.append(jnp.where(behind == jnp.asarray(k, jnp.bfloat16), value, zero))
        for sub in range(0, SIDE, 2):
            high = jnp.where(first_half, highs[sub], highs[sub + 1]).astype(jnp.bfloat16)
            masked.append(jnp.where(high_ids == high, one, zero))
        result = dot_nt(jnp.concatenate(masked, axis=0), jnp.concatenate(weights, axis=0))
        found = []
        for sub in range(SIDE):
            start = sub * HIGH * sub_width
            tally = result[SIDE * HIGH * sub_width + sub * HIGH :][:HIGH]
            halves, tallies = [], []
            for first in range(0, HIGH, spots):
                total, counted = None, None
                for k in range(first, first + spots):
                    piece = part(result[start + k * sub_width :][:sub_width], sub, k)
                    total = piece if total is None else jnp.where(spot == k % spots, piece, total)
                    piece = jnp.where(line == k, part(tally, sub, k), 0.0)
                    counted = piece if counted is None else jnp.where(spot == k % spots, piece, counted)
                halves.append(total)
                tallies.append(jnp.sum(counted, axis=0, keepdims=True))
            found.append((halves, tallies))
        return found

    pending, done = [], 0
    for share in range(shares):
        if share:
            notes[share].wait()
        correct(share)
        for base in range(starts[share], ends[share], SIDE):
            pending += spread(base)
            while len(pending) >= GROUP:
                lines = [jnp.concatenate(halves, axis=1) for halves, _ in pending[:GROUP]]
                tally = jnp.zeros((8, CODEWORDS), jnp.float32)
                for place, (_, tallies) in enumerate(pending[:GROUP]):
                    row = jnp.broadcast_to(jnp.concatenate(tallies, axis=1), (8, CODEWORDS))
                    tally = jnp.where(wide_line == place, row, tally)
                out_ref[done] = jnp.concatenate(lines + [tally], axis=0).astype(jnp.bfloat16)
                pending, done = pending[GROUP:], done + 1
    store.wait()


def whole(count):
    return [pl.BlockSpec(memory_space=pltpu.VMEM)] * count


def anywhere(count):
    return [pl.BlockSpec(memory_space=pl.ANY)] * count


def shaped(shape, kind=jnp.float32):
    return jax.ShapeDtypeStruct(shape, kind)


def body(child_centroids, child_sizes, parent_of, points, assign, codes, rotation):
    lists, rings = lax.axis_size("lists"), lax.axis_size("z")
    chips = lists * rings
    core = lax.axis_index("core")
    child_count, width = child_centroids.shape
    count, subspaces = codes.shape
    owner_parents = rings * child_count
    shard_rows = child_count // 2
    most = child_count // math.isqrt(lists)
    wide = width + LANES

    packed = pl.pallas_call(
        functools.partial(pack_kernel, owner_parents),
        out_shape=shaped((lists, rings, most, width), jnp.int16),
        in_specs=anywhere(3),
        out_specs=whole(1)[0],
        scratch_shapes=[
            pltpu.VMEM((child_count, width), jnp.float32),
            pltpu.VMEM((1, child_count), jnp.int32),
            pltpu.VMEM((1, child_count), jnp.int32),
            pltpu.SemaphoreType.DMA((3,)),
        ],
        compiler_params=pltpu.CompilerParams(vmem_limit_bytes=FULL),
    )(child_centroids, child_sizes[None, :], parent_of[None, :])
    near = lax.all_to_all(packed.reshape(chips, most, width), ("lists", "z"), 0, 0)
    half_width, half_subspaces, pair_count = width // 2, subspaces // 2, 2 * count
    turned_codes, parent_row = codes.T, assign[None, :]

    def both(array):
        return array, lax.ppermute(array, "core", SWAP)

    first = SHARES[0] * SIDE
    early_rows = first * (width // subspaces) + 2 * first + 8
    rotated, early, turned = pl.pallas_call(
        rotate_kernel,
        out_shape=(
            shaped((SLABS, half_width, pair_count)),
            shaped((early_rows, pair_count)),
            shaped((half_width, width), jnp.bfloat16),
        ),
        in_specs=anywhere(7),
        out_specs=tuple(anywhere(3)),
        scratch_shapes=[
            pltpu.VMEM((pair_count, width), jnp.bfloat16),
            pltpu.VMEM((2, subspaces, count), jnp.int32),
            pltpu.VMEM((2, 1, count), jnp.int32),
            pltpu.VMEM((width, width), jnp.bfloat16),
            pltpu.VMEM((half_width, pair_count), jnp.float32),
            pltpu.VMEM((half_width, width), jnp.bfloat16),
            pltpu.VMEM((subspaces + 8, pair_count), jnp.float32),
            pltpu.SemaphoreType.DMA((2 * PIECES + 5,)),
            pltpu.SemaphoreType.DMA((4 * PIECES + 4,)),
        ],
        compiler_params=pltpu.CompilerParams(vmem_limit_bytes=MOST),
        cost_estimate=pl.CostEstimate(flops=2 * width * width * count, bytes_accessed=14 << 20, transcendentals=0),
    )(*both(points), *both(turned_codes), *both(parent_row), rotation)
    mine = pl.pallas_call(
        merge_kernel,
        out_shape=shaped((owner_parents, wide)),
        in_specs=whole(1) + anywhere(1),
        out_specs=whole(1)[0],
        compiler_params=pltpu.CompilerParams(vmem_limit_bytes=SOME),
    )(near.reshape(chips * most, width), rotated)
    sums_of_list = mine + lax.ppermute(mine, "core", SWAP)
    groups = half_subspaces // GROUP
    rows = GROUP * (width // subspaces) + 8
    sums, merged = pl.pallas_call(
        code_kernel,
        out_shape=(shaped((groups, rows, CODEWORDS), jnp.bfloat16), shaped((shard_rows, width))),
        in_specs=whole(3) + anywhere(1),
        out_specs=tuple(whole(1) + anywhere(1)),
        scratch_shapes=[
            pltpu.VMEM((owner_parents, width), jnp.float32),
            pltpu.VMEM((half_width, pair_count), jnp.float32),
            pltpu.VMEM((2 * owner_parents, pair_count), jnp.bfloat16),
            pltpu.VMEM((subspaces + 8, pair_count), jnp.float32),
            pltpu.SemaphoreType.DMA((2 * len(SHARES),)),
        ],
        compiler_params=pltpu.CompilerParams(vmem_limit_bytes=SOME),
    )(sums_of_list, early, turned, rotated)

    splits = chips // groups
    chip = sums.reshape(groups, rows, splits, CODEWORDS // splits)
    chip = chip.transpose(0, 2, 1, 3).reshape(chips, rows, CODEWORDS // splits)
    total = jnp.sum(lax.all_to_all(chip, ("lists", "z"), 0, 0).astype(jnp.float32), axis=0)
    sub_width = (rows - 8) // GROUP
    tops = total[: rows - 8].reshape(GROUP, sub_width, -1)
    means = tops / (1.0 + total[rows - 8 : rows - 8 + GROUP, None, :])
    means = means.reshape(1, rows - 8, -1).astype(jnp.bfloat16)
    means = jnp.broadcast_to(means, (chips,) + means.shape[1:])
    mine = lax.all_to_all(means, ("lists", "z"), 0, 0)
    mine = mine.reshape(groups, splits, rows - 8, -1).transpose(0, 2, 1, 3).reshape(-1, CODEWORDS)
    other = lax.ppermute(mine, "core", SWAP)
    first = core == 0
    means = jnp.concatenate([jnp.where(first, mine, other), jnp.where(first, other, mine)], axis=0)
    return merged, means.astype(jnp.float32)


def solution(mesh):
    lists, points = mesh.devices.shape
    split = jax.sharding.Mesh(mesh.devices.reshape(lists, points // 2, 2), ("lists", "z", "core"))
    every = ("lists", "z", "core")
    in_specs = (P(every, None), P(every), P(every), P(every, None), P(every), P(every, None), P())
    out_specs = (P(every, None), P())
    return jax.shard_map(body, mesh=split, in_specs=in_specs, out_specs=out_specs, check_vma=False)
```

```python
import functools
import math

import jax
import jax.numpy as jnp
from jax import lax
from jax.experimental import pallas as pl
from jax.experimental.pallas import tpu as pltpu
from jax.sharding import PartitionSpec as P

CODEWORDS = 256
LOW = 32
HIGH = CODEWORDS // LOW
GROUP = 3
SIDE = 8
SHARES = (2, 4)
FRACTION = 14.0
SIZE_BITS, PARENT_BITS, EXPONENT_BITS = 9, 13, 8
SLABS = 4
PIECES = 3
LANES = 128

FULL = 66_900_000
MOST = 66_200_000
SOME = 50_000_000
SWAP = ((0, 1), (1, 0))


def dot_nt(a, b):
    return lax.dot_general(a, b, (((1,), (1,)), ((), ())), preferred_element_type=jnp.float32)


def as_column(row):
    count = row.shape[1]
    shape = (count, count)
    here = lax.broadcasted_iota(jnp.int32, shape, 0) == lax.broadcasted_iota(jnp.int32, shape, 1)
    return jnp.sum(jnp.where(here, jnp.broadcast_to(row, shape), 0), axis=1, keepdims=True)


def power(exponent):
    return jnp.exp2(exponent)


def pack_kernel(owner_parents, child_hbm, size_hbm, parent_hbm, out_ref, child_ref, size_ref, parent_ref, sems):
    copies = [
        pltpu.make_async_copy(source, target, sems.at[k])
        for k, (source, target) in enumerate(
            ((child_hbm, child_ref), (size_hbm, size_ref), (parent_hbm, parent_ref))
        )
    ]
    for copy in copies:
        copy.start()
    for copy in copies:
        copy.wait()
    lists, rings, most, width = out_ref.shape
    count = child_ref.shape[0]
    parent_row = parent_ref[...]
    parent = as_column(parent_row)
    size = as_column(size_ref[...])
    owner_row, owner = parent_row // owner_parents, parent // owner_parents
    shape = (count, count)
    before = lax.broadcasted_iota(jnp.int32, shape, 0) < lax.broadcasted_iota(jnp.int32, shape, 1)
    earlier = jnp.where((owner == owner_row) & before, 1, 0)
    slot = owner_row * most + jnp.sum(earlier, axis=0, keepdims=True)
    slots = lax.broadcasted_iota(jnp.int32, (lists * most, count), 0)
    pack = jnp.where(slots == slot, 1.0, 0.0).astype(jnp.bfloat16)
    child = child_ref[...]
    top = jnp.max(jnp.abs(child), axis=1, keepdims=True)
    exponent = jnp.ceil(jnp.log2(jnp.maximum(top, 1e-30)))
    scaled = jnp.floor(child * power(FRACTION - exponent) + 0.5)
    word = size + (parent << SIZE_BITS)
    word = word + ((exponent.astype(jnp.int32) + 128) << (SIZE_BITS + PARENT_BITS))
    lane = lax.broadcasted_iota(jnp.int32, (count, LANES), 1)
    bit = (jnp.broadcast_to(word, (count, LANES)) >> jnp.minimum(lane, 31)) & 1
    marked = 2.0 * jnp.floor(scaled[:, :LANES] * 0.5) + bit.astype(jnp.float32)
    sent = jnp.concatenate([marked, scaled[:, LANES:]], axis=1)
    upper = jnp.floor(sent * (1.0 / 128.0))
    lower = sent - upper * 128.0
    packed = 128.0 * jnp.dot(pack, upper.astype(jnp.bfloat16), preferred_element_type=jnp.float32)
    packed = packed + jnp.dot(pack, lower.astype(jnp.bfloat16), preferred_element_type=jnp.float32)
    for k in range(lists):
        block = packed[k * most : (k + 1) * most].astype(jnp.int32).astype(jnp.int16)
        for ring in range(rings):
            out_ref[k, ring] = block


def merge_kernel(near_ref, after_ref, out_ref):
    del after_ref
    parents = out_ref.shape[0]
    first = lax.axis_index("lists") * parents
    width = out_ref.shape[1] - LANES
    near = near_ref[...].astype(jnp.int32)
    bits = (near[:, :LANES] & 1).astype(jnp.float32).astype(jnp.bfloat16)
    shape = (LANES, LANES)
    line, lane = lax.broadcasted_iota(jnp.int32, shape, 0), lax.broadcasted_iota(jnp.int32, shape, 1)
    values = jnp.zeros(shape, jnp.float32)
    start = 0
    for k, length in enumerate((SIZE_BITS, PARENT_BITS, EXPONENT_BITS)):
        keep = (lane == k) & (line >= start) & (line < start + length)
        value = (1 << jnp.minimum(jnp.maximum(line - start, 0), length)).astype(jnp.float32)
        values = jnp.where(keep, value, values)
        start += length
    note = jnp.dot(bits, values.astype(jnp.bfloat16), preferred_element_type=jnp.float32)
    size, parent, exponent = note[:, 0:1], note[:, 1:2], note[:, 2:3] - 128.0
    wanted = (lax.broadcasted_iota(jnp.int32, (near.shape[0], parents), 1) + first).astype(jnp.float32)
    pick = jnp.where(parent == wanted, 1.0, 0.0).astype(jnp.bfloat16)
    value = near.astype(jnp.float32) * (size * power(exponent - FRACTION))
    upper = value.astype(jnp.bfloat16)
    lower = (value - upper.astype(jnp.float32)).astype(jnp.bfloat16)

    def picked(rows):
        return lax.dot_general(pick, rows, (((0,), (0,)), ((), ())), preferred_element_type=jnp.float32)

    out_ref[:, :width] = picked(upper) + picked(lower)
    lane = lax.broadcasted_iota(jnp.int32, note.shape, 1)
    out_ref[:, width:] = picked(jnp.where(lane == 0, size, 0.0).astype(jnp.bfloat16))


def rotate_kernel(
    points_hbm, points_other_hbm, codes_hbm, codes_other_hbm, assign_hbm, assign_other_hbm, rotation_hbm,
    out_hbm, early_hbm, turned_hbm,
    points_ref, codes_ref, assign_ref, assign_other_ref, rotation_ref, out_ref, turned_ref, note_ref, in_sems, out_sems,
):
    width, count = out_ref.shape
    own = count // 2
    subspaces = codes_ref.shape[1] // 2
    piece = own // PIECES
    core = lax.axis_index("core")
    first = pl.multiple_of(core * width, LANES)
    fetch = pltpu.make_async_copy(rotation_hbm, rotation_ref, in_sems.at[0])
    fetch.start()
    fetches = []
    for side, source in enumerate((points_hbm, points_other_hbm)):
        for k in range(PIECES):
            part = slice(k * piece, (k + 1) * piece)
            target = points_ref.at[side * own + k * piece : side * own + (k + 1) * piece]
            fetches.append(pltpu.make_async_copy(source.at[part], target, in_sems.at[1 + side * PIECES + k]))
    notes = []
    for k, (source, target) in enumerate(
        (
            (codes_hbm, codes_ref.at[0]),
            (codes_other_hbm, codes_ref.at[1]),
            (assign_hbm, assign_ref),
            (assign_other_hbm, assign_other_ref),
        )
    ):
        notes.append(pltpu.make_async_copy(source, target, in_sems.at[1 + 2 * PIECES + k]))
    for copy in fetches + notes:
        copy.start()
    fetch.wait()
    turned_ref[...] = rotation_ref[:, pl.ds(first, width)].T
    early = SHARES[0] * SIDE * (width // subspaces)
    stores = [pltpu.make_async_copy(turned_ref, turned_hbm, out_sems.at[4 * PIECES])]
    stores[0].start()
    for k in range(2 * PIECES):
        part = slice(k * piece, (k + 1) * piece)
        fetches[k].wait()
        out_ref[:, part] = dot_nt(turned_ref[...], points_ref[part, :])
        for j, (source, target) in enumerate(
            (
                (out_ref.at[:early, part], early_hbm.at[:early, part]),
                (out_ref.at[early:, part], out_hbm.at[0, early:, part]),
            )
        ):
            store = pltpu.make_async_copy(source, target, out_sems.at[2 * k + j])
            store.start()
            stores.append(store)
    for copy in notes:
        copy.wait()
    chosen = pl.ds(pl.multiple_of(core * subspaces, 8), subspaces)
    for side in range(2):
        part = slice(side * own, (side + 1) * own)
        code = codes_ref[side, chosen, :]
        low, high = (code & (LOW - 1)).astype(jnp.float32), (code // LOW).astype(jnp.float32)
        for start in range(0, subspaces, SIDE):
            note_ref[2 * start : 2 * start + SIDE, part] = low[start : start + SIDE]
            note_ref[2 * start + SIDE : 2 * (start + SIDE), part] = high[start : start + SIDE]
        note_ref[2 * subspaces :, part] = jnp.broadcast_to(
            (assign_ref, assign_other_ref)[side][...].reshape(1, own).astype(jnp.float32), (8, own)
        )
    lines, after = 2 * SHARES[0] * SIDE, 2 * subspaces
    for k, (source, target) in enumerate(
        (
            (note_ref.at[:lines], early_hbm.at[early : early + lines]),
            (note_ref.at[after:], early_hbm.at[early + lines :]),
            (note_ref.at[lines:after], out_hbm.at[1, lines:after]),
        )
    ):
        store = pltpu.make_async_copy(source, target, out_sems.at[4 * PIECES + 1 + k])
        store.start()
        stores.append(store)
    for store in stores:
        store.wait()


def code_kernel(
    whole_ref, early_ref, turned_ref, rotated_hbm, out_ref, merged_hbm, all_ref, rot_ref, pick_ref, note_ref, sems
):
    width, count = rot_ref.shape
    parents, columns = all_ref.shape
    subspaces = out_ref.shape[0] * GROUP
    sub_width = width // subspaces
    shares = len(SHARES)
    ends = [sum(SHARES[: k + 1]) * SIDE for k in range(shares)]
    starts = [0] + ends[:-1]
    early = ends[0] * sub_width

    def columns_of(share):
        return slice(starts[share] * sub_width, ends[share] * sub_width)

    fetches, notes = [None], [None]
    for share in range(1, shares):
        span = columns_of(share)
        fetches.append(pltpu.make_async_copy(rotated_hbm.at[0, span], rot_ref.at[span], sems.at[share]))
        span = slice(2 * starts[share], 2 * ends[share])
        notes.append(pltpu.make_async_copy(rotated_hbm.at[1, span], note_ref.at[span], sems.at[shares + share]))
        fetches[share].start()
        notes[share].start()
    all_ref[...] = whole_ref[:, :columns] / whole_ref[:, columns : columns + 1]
    shard_rows = merged_hbm.shape[0]
    shard = lax.axis_index("z") * 2 + lax.axis_index("core")
    mine = all_ref.at[pl.ds(pl.multiple_of(shard * shard_rows, shard_rows), shard_rows)]
    store = pltpu.make_async_copy(mine, merged_hbm, sems.at[0])
    store.start()
    lowered = all_ref[...].astype(jnp.bfloat16)
    ids = lax.broadcasted_iota(jnp.int32, (parents, count), 0).astype(jnp.float32)
    pick = jnp.where(ids == early_ref[early + 2 * ends[0] : early + 2 * ends[0] + 1, :], 1.0, 0.0).astype(jnp.bfloat16)
    pick_ref[:parents, :] = pick
    pick_ref[parents:, :] = pick
    piece = count // (2 * PIECES)

    def correct(share):
        span = columns_of(share)
        parent = dot_nt(turned_ref[span, :], lowered)
        upper = parent.astype(jnp.bfloat16)
        lower = (parent - upper.astype(jnp.float32)).astype(jnp.bfloat16)
        both = jnp.concatenate([upper, lower], axis=1)
        if share:
            fetches[share].wait()
        source = rot_ref if share else early_ref
        for k in range(2 * PIECES):
            part = slice(k * piece, (k + 1) * piece)
            chosen = jnp.dot(both, pick_ref[:, part], preferred_element_type=jnp.float32)
            rot_ref[span, part] = source[span, part] - chosen

    def small(ids):
        return ids.astype(jnp.float32).astype(jnp.bfloat16)

    tile = 2 * sub_width
    low_ids = [small(lax.broadcasted_iota(jnp.int32, (tile, count), 0) + start) for start in range(0, LOW, tile)]
    pair_ids = small(lax.broadcasted_iota(jnp.int32, (tile, count), 0) // sub_width)
    high_ids = small(lax.broadcasted_iota(jnp.int32, (tile, count), 0) % HIGH)
    first_half = lax.broadcasted_iota(jnp.int32, (tile, count), 0) < HIGH
    spot = lax.broadcasted_iota(jnp.int32, (8, LANES), 1) // LOW
    line = lax.broadcasted_iota(jnp.int32, (8, LANES), 0)
    one, zero = jnp.ones((), jnp.bfloat16), jnp.zeros((), jnp.bfloat16)
    spots = LANES // LOW

    def part(rows, sub, place):
        rows = rows[:, sub // spots * LANES : (sub // spots + 1) * LANES]
        turn = (place - sub) % spots * LOW
        return pltpu.roll(rows, turn, 1) if turn else rows

    def spread(base):
        weights, masked, highs = [], [], []
        note = note_ref if base >= ends[0] else early_ref.at[early:]
        for sub in range(SIDE):
            index = base + sub
            low = jnp.broadcast_to(note[2 * base + sub : 2 * base + sub + 1, :], (tile, count)).astype(jnp.bfloat16)
            weights += [jnp.where(ids == low, one, zero) for ids in low_ids]
            value = rot_ref[index * sub_width : (index + 1) * sub_width, :]
            value = jnp.concatenate([value, value], axis=0).astype(jnp.bfloat16)
            high = jnp.broadcast_to(note[2 * base + SIDE + sub : 2 * base + SIDE + sub + 1, :], (tile, count))
            highs.append(high)
            behind = high.astype(jnp.bfloat16) - pair_ids
            for k in range(0, HIGH, 2):
                masked.append(jnp.where(behind == jnp.asarray(k, jnp.bfloat16), value, zero))
        for sub in range(0, SIDE, 2):
            high = jnp.where(first_half, highs[sub], highs[sub + 1]).astype(jnp.bfloat16)
            masked.append(jnp.where(high_ids == high, one, zero))
        result = dot_nt(jnp.concatenate(masked, axis=0), jnp.concatenate(weights, axis=0))
        found = []
        for sub in range(SIDE):
            start = sub * HIGH * sub_width
            tally = result[SIDE * HIGH * sub_width + sub * HIGH :][:HIGH]
            halves, tallies = [], []
            for first in range(0, HIGH, spots):
                total, counted = None, None
                for k in range(first, first + spots):
                    piece = part(result[start + k * sub_width :][:sub_width], sub, k)
                    total = piece if total is None else jnp.where(spot == k % spots, piece, total)
                    piece = jnp.where(line == k, part(tally, sub, k), 0.0)
                    counted = piece if counted is None else jnp.where(spot == k % spots, piece, counted)
                halves.append(total)
                tallies.append(jnp.sum(counted, axis=0, keepdims=True))
            found.append((halves, tallies))
        return found

    pending, done = [], 0
    for share in range(shares):
        if share:
            notes[share].wait()
        correct(share)
        for base in range(starts[share], ends[share], SIDE):
            pending += spread(base)
            while len(pending) >= GROUP:
                lines = [halves[side] for side in range(2) for halves, _ in pending[:GROUP]]
                tally = jnp.zeros((8, LANES), jnp.float32)
                for place in range(2 * GROUP):
                    row = pending[place % GROUP][1][place // GROUP]
                    tally = jnp.where(line == place, jnp.broadcast_to(row, (8, LANES)), tally)
                out_ref[done] = jnp.concatenate(lines + [tally], axis=0).astype(jnp.bfloat16)
                pending, done = pending[GROUP:], done + 1
    store.wait()


def whole(count):
    return [pl.BlockSpec(memory_space=pltpu.VMEM)] * count


def anywhere(count):
    return [pl.BlockSpec(memory_space=pl.ANY)] * count


def shaped(shape, kind=jnp.float32):
    return jax.ShapeDtypeStruct(shape, kind)


def body(child_centroids, child_sizes, parent_of, points, assign, codes, rotation):
    lists, rings = lax.axis_size("lists"), lax.axis_size("z")
    chips = lists * rings
    core = lax.axis_index("core")
    child_count, width = child_centroids.shape
    count, subspaces = codes.shape
    owner_parents = rings * child_count
    shard_rows = child_count // 2
    most = child_count // math.isqrt(lists)
    wide = width + LANES

    packed = pl.pallas_call(
        functools.partial(pack_kernel, owner_parents),
        out_shape=shaped((lists, rings, most, width), jnp.int16),
        in_specs=anywhere(3),
        out_specs=whole(1)[0],
        scratch_shapes=[
            pltpu.VMEM((child_count, width), jnp.float32),
            pltpu.VMEM((1, child_count), jnp.int32),
            pltpu.VMEM((1, child_count), jnp.int32),
            pltpu.SemaphoreType.DMA((3,)),
        ],
        compiler_params=pltpu.CompilerParams(vmem_limit_bytes=FULL),
    )(child_centroids, child_sizes[None, :], parent_of[None, :])
    near = lax.all_to_all(packed.reshape(chips, most, width), ("lists", "z"), 0, 0)
    half_width, half_subspaces, pair_count = width // 2, subspaces // 2, 2 * count
    turned_codes, parent_row = codes.T, assign

    def both(array):
        return array, lax.ppermute(array, "core", SWAP)

    first = SHARES[0] * SIDE
    early_rows = first * (width // subspaces) + 2 * first + 8
    rotated, early, turned = pl.pallas_call(
        rotate_kernel,
        out_shape=(
            shaped((SLABS, half_width, pair_count)),
            shaped((early_rows, pair_count)),
            shaped((half_width, width), jnp.bfloat16),
        ),
        in_specs=anywhere(7),
        out_specs=tuple(anywhere(3)),
        scratch_shapes=[
            pltpu.VMEM((pair_count, width), jnp.bfloat16),
            pltpu.VMEM((2, subspaces, count), jnp.int32),
            pltpu.VMEM((count,), jnp.int32),
            pltpu.VMEM((count,), jnp.int32),
            pltpu.VMEM((width, width), jnp.bfloat16),
            pltpu.VMEM((half_width, pair_count), jnp.float32),
            pltpu.VMEM((half_width, width), jnp.bfloat16),
            pltpu.VMEM((subspaces + 8, pair_count), jnp.float32),
            pltpu.SemaphoreType.DMA((2 * PIECES + 5,)),
            pltpu.SemaphoreType.DMA((4 * PIECES + 4,)),
        ],
        compiler_params=pltpu.CompilerParams(vmem_limit_bytes=MOST),
        cost_estimate=pl.CostEstimate(flops=2 * width * width * count, bytes_accessed=14 << 20, transcendentals=0),
    )(*both(points), *both(turned_codes), *both(parent_row), rotation)
    mine = pl.pallas_call(
        merge_kernel,
        out_shape=shaped((owner_parents, wide)),
        in_specs=whole(1) + anywhere(1),
        out_specs=whole(1)[0],
        compiler_params=pltpu.CompilerParams(vmem_limit_bytes=SOME),
    )(near.reshape(chips * most, width), rotated)
    sums_of_list = mine + lax.ppermute(mine, "core", SWAP)
    groups = half_subspaces // GROUP
    tops = GROUP * (width // subspaces)
    rows = 2 * tops + 8
    sums, merged = pl.pallas_call(
        code_kernel,
        out_shape=(shaped((groups, rows, LANES), jnp.bfloat16), shaped((shard_rows, width))),
        in_specs=whole(3) + anywhere(1),
        out_specs=tuple(whole(1) + anywhere(1)),
        scratch_shapes=[
            pltpu.VMEM((owner_parents, width), jnp.float32),
            pltpu.VMEM((half_width, pair_count), jnp.float32),
            pltpu.VMEM((2 * owner_parents, pair_count), jnp.bfloat16),
            pltpu.VMEM((subspaces + 8, pair_count), jnp.float32),
            pltpu.SemaphoreType.DMA((2 * len(SHARES),)),
        ],
        compiler_params=pltpu.CompilerParams(vmem_limit_bytes=SOME),
    )(sums_of_list, early, turned, rotated)

    splits = chips // groups
    part = LANES // splits
    chip = sums.reshape(groups, rows, splits, part).transpose(0, 2, 1, 3).reshape(chips, rows, part)
    total = jnp.sum(lax.all_to_all(chip, ("lists", "z"), 0, 0).astype(jnp.float32), axis=0)
    counts = total[2 * tops : 2 * tops + 2 * GROUP].reshape(2, GROUP, 1, part)
    means = total[: 2 * tops].reshape(2, GROUP, tops // GROUP, part) / (1.0 + counts)
    means = means.reshape(2, tops, part).astype(jnp.bfloat16)
    means = jnp.concatenate([means[0], means[1]], axis=1)
    means = jnp.broadcast_to(means[None], (chips, tops, 2 * part))
    mine = lax.all_to_all(means, ("lists", "z"), 0, 0)
    if splits > 1:
        mine = mine.reshape(groups, splits, tops, 2, part).transpose(0, 2, 3, 1, 4)
    mine = mine.reshape(groups * tops, CODEWORDS)
    other = lax.ppermute(mine, "core", SWAP)
    first = core == 0
    means = jnp.concatenate([jnp.where(first, mine, other), jnp.where(first, other, mine)], axis=0)
    return merged, means.astype(jnp.float32)


def solution(mesh):
    lists, points = mesh.devices.shape
    split = jax.sharding.Mesh(mesh.devices.reshape(lists, points // 2, 2), ("lists", "z", "core"))
    every = ("lists", "z", "core")
    in_specs = (P(every, None), P(every), P(every), P(every, None), P(every), P(every, None), P())
    out_specs = (P(every, None), P())
    return jax.shard_map(body, mesh=split, in_specs=in_specs, out_specs=out_specs, check_vma=False)
```
